256 devices in a mesh: boxgrp: 64 (over z, y, core), sub: 4 (over x).
Axes of the slice: x: 4, y: 4, z: 8, core: 2. Of those that a mesh axis runs over, the one named last changes fastest.
Arguments:
- coarse_velocity: float32 [3, 1024, 64, 32], P(None, ('boxgrp', 'sub')), may hold values from -6 to 6
- coarse_pressure: float32 [1024, 64, 32], P(('boxgrp', 'sub')), may hold values from -6 to 6
- coarse_viscosity: float32 [1024, 64, 32], P(('boxgrp', 'sub')), may hold values from 0.1 to 10
- coarse_force: float32 [3, 1024, 64, 32], P(None, ('boxgrp', 'sub')), may hold values from -6 to 6
- refined_velocity_field: float32 [3, 32, 64, 64, 64], P(None, 'sub', 'boxgrp'), may hold values from -6 to 6
- refined_pressure_field: float32 [32, 64, 64, 64], P('sub', 'boxgrp'), may hold values from -6 to 6
- refined_viscosity_field: float32 [32, 64, 64, 64], P('sub', 'boxgrp'), may hold values from 0.1 to 10
- refined_body_force: float32 [3, 32, 64, 64, 64], P(None, 'sub', 'boxgrp'), may hold values from -6 to 6
- box_spots: int32 [64], replicated, may hold values from -1 to 1, as said below
Outputs:
- new_coarse_velocity: float32 [3, 1024, 64, 32], P(None, ('boxgrp', 'sub'))
- new_coarse_pressure: float32 [1024, 64, 32], P(('boxgrp', 'sub'))
- new_fine_velocity: float32 [3, 32, 64, 64, 64], P(None, 'sub', 'boxgrp')
- new_fine_pressure: float32 [32, 64, 64, 64], P('sub', 'boxgrp')
The draws below stay inside these ranges and needn't reach their ends.
Inputs may be any that keep to these rules, and one draw needn't show every extreme that they name: `box_spots`: slot j belongs to group j and holds the place q (0 or 1) of its fine box along y in that group's slab, or -1 if the slot is empty. The places of one group differ, two consecutive groups share no place, and some group fills all 1 slots.
All inputs are finite; a program needn't handle non-finite values.
Results may differ from the reference program's by a relative error of at most 0.0003.
Values sent between devices are 32-bit elements; how exact they have to be, the bound alone decides.
A program may use at most 64 MiB of HBM per device.

```python
import math
from functools import partial
from functools import reduce
import jax
import jax.numpy as jnp
from jax import lax

FINE_CELLS_Y = 64
FINE_CELLS_X = 64
YSPOTS = 2
XSPOTS = 1
SWEEPS = 2
FINE_CELLS_Z = 32
FSLOT = 1
BOX_SLOT_COUNT = 64
NZ = 1024
NY = 64
NX = 32
N_BOXGRP = 64


def draw_box_spots(key, part):
    spot_total = YSPOTS * XSPOTS
    key_count, key_full, key_groups = jax.random.split(jax.random.fold_in(key, 7), 3)
    counts_all = jax.random.randint(key_count, (N_BOXGRP,), 0, FSLOT + 1)
    full_group = jax.random.randint(key_full, (), 0, N_BOXGRP)
    counts_all = jnp.where(jnp.arange(N_BOXGRP) == full_group, FSLOT, counts_all)

    def choose(previous, inputs):
        group_key, count_here = inputs
        key_score, key_order = jax.random.split(group_key)
        places = jnp.arange(spot_total, dtype=jnp.int32)
        scores = jax.random.randint(key_score, (spot_total,), 0, 1024) * spot_total + places
        scores = jnp.where(previous, -1 - places, scores)
        ranking = jnp.argsort(-scores, stable=True).astype(jnp.int32)
        rank_of = jnp.argsort(ranking, stable=True)
        chosen = rank_of < count_here
        slot_order = jax.random.permutation(key_order, FSLOT)
        picked = jnp.where(slot_order < count_here, ranking[slot_order], -1)
        return (chosen, picked.astype(jnp.int32))
    group_keys = jax.random.split(key_groups, N_BOXGRP)
    unused_last, spots_all = lax.scan(choose, jnp.zeros((spot_total,), jnp.bool_), (group_keys, counts_all))
    return spots_all.reshape(-1).astype(jnp.int32)


def shard_levels(stream_key, shape, shards, least, top_value):
    def one(position, shards_of):
        draws = jax.random.uniform(jax.random.fold_in(jax.random.fold_in(stream_key, 6), position), (shards_of,), jnp.float32, least / len(shards), top_value / len(shards))
        return jnp.repeat(jnp.exp(draws), shape[position] // shards_of).reshape((-1,) + (1,) * (len(shape) - position - 1))

    factor_of = one(*shards[0])
    for cut in shards[1:]:
        factor_of = factor_of * one(*cut)
    return factor_of


def centred(key, extent, scale, most, shards=(), kind=jnp.bfloat16):
    drawn = jax.random.normal(key, extent, jnp.float32) * scale
    if len(shards) > 0:
        drawn = shard_levels(key, extent, shards, -0.22, 0.18) * drawn
    return jnp.clip(drawn, min=-most, max=most).astype(kind)


def setup_inputs(seed: int = 0) -> dict:
    arg_keys = jax.random.split(jax.random.key(seed), 10)
    coarse_velocity = centred(arg_keys[0], (3, NZ, NY, NX), 1.0, 6.0, ((1, 256),), jnp.float32)
    coarse_pressure = centred(arg_keys[1], (NZ, NY, NX), 1.0, 6.0, ((0, 256),), jnp.float32)
    coarse_viscosity = jnp.clip(jnp.exp(math.log(10.0) - 4.6051702 * jax.random.uniform(arg_keys[2], (NZ, NY, NX), jnp.float32) ** shard_levels(arg_keys[2], (NZ, NY, NX), ((0, 256),), -0.2, 0.2)), 0.1, 10.0)
    coarse_force = centred(arg_keys[3], (3, NZ, NY, NX), 1.0, 6.0, ((1, 256),), jnp.float32)
    refined_velocity_field = centred(arg_keys[4], (3, FINE_CELLS_Z, BOX_SLOT_COUNT, FINE_CELLS_Y, FINE_CELLS_X), 1.0, 6.0, ((1, 4), (2, 64)), jnp.float32)
    refined_pressure_field = centred(arg_keys[5], (FINE_CELLS_Z, BOX_SLOT_COUNT, FINE_CELLS_Y, FINE_CELLS_X), 1.0, 6.0, ((0, 4), (1, 64)), jnp.float32)
    refined_viscosity_field = jnp.clip(jnp.exp(math.log(10.0) - 4.6051702 * jax.random.uniform(arg_keys[6], (FINE_CELLS_Z, BOX_SLOT_COUNT, FINE_CELLS_Y, FINE_CELLS_X), jnp.float32) ** shard_levels(arg_keys[6], (FINE_CELLS_Z, BOX_SLOT_COUNT, FINE_CELLS_Y, FINE_CELLS_X), ((0, 4), (1, 64)), -0.2, 0.2)), 0.1, 10.0)
    refined_body_force = centred(arg_keys[7], (3, FINE_CELLS_Z, BOX_SLOT_COUNT, FINE_CELLS_Y, FINE_CELLS_X), 1.0, 6.0, ((1, 4), (2, 64)), jnp.float32)
    box_spots = draw_box_spots(jax.random.fold_in(arg_keys[9], 71), 0)
    return {"coarse_velocity": coarse_velocity, "coarse_pressure": coarse_pressure, "coarse_viscosity": coarse_viscosity, "coarse_force": coarse_force, "refined_velocity_field": refined_velocity_field, "refined_pressure_field": refined_pressure_field, "refined_viscosity_field": refined_viscosity_field, "refined_body_force": refined_body_force, "box_spots": box_spots}


RELAX_SCALE = 1.25
DAMPING = 0.8
PRECISE = lax.Precision.HIGHEST


def add_all(terms):
    return reduce(lambda left_v, right_v: left_v + right_v, terms)


def center(field_in, planes):
    start_at = (field_in.shape[1] - planes) // 2
    return lax.slice_in_dim(field_in, start_at, start_at + planes, axis=1)


def beside_all(padded):
    middle = padded[:, 1:-1, :, 1:-1, 1:-1]
    beside = [padded[:, :-2, :, 1:-1, 1:-1], padded[:, 2:, :, 1:-1, 1:-1],
              padded[:, 1:-1, :, :-2, 1:-1], padded[:, 1:-1, :, 2:, 1:-1],
              padded[:, 1:-1, :, 1:-1, :-2], padded[:, 1:-1, :, 1:-1, 2:]]
    return middle, beside


def divergence(beside, inv_two):
    return ((beside[1][0:1] - beside[0][0:1]) + (beside[3][1:2] - beside[2][1:2])
            + (beside[5][2:3] - beside[4][2:3])) * inv_two


def gradient(beside, inv_two):
    return jnp.concatenate([beside[1] - beside[0], beside[3] - beside[2], beside[5] - beside[4]], 0) * inv_two


def first_section(padded, force, inv_sq, inv_two):
    mu_mid, mu_beside = beside_all(padded[4:5])
    mu_faces = [0.5 * (mu_mid + nearby) for nearby in mu_beside]
    diag_a = inv_sq * add_all(mu_faces)
    vel_mid, vel_beside = beside_all(padded[0:3])
    apply_a = inv_sq * add_all([mu_face * (vel_mid - nearby) for mu_face, nearby in zip(mu_faces, vel_beside)])
    pres_mid, pres_beside = beside_all(padded[3:4])
    resid_u = force - apply_a - gradient(pres_beside, inv_two)
    resid_p = -divergence(vel_beside, inv_two)
    relaxed = resid_u / (RELAX_SCALE * diag_a)
    return relaxed, diag_a, resid_p


def second_section(padded, resid_p, inv_sq, inv_two):
    rel_mid, rel_beside = beside_all(padded[0:3])
    source = resid_p - divergence(rel_beside, inv_two)
    diag_mid, diag_beside = beside_all(padded[3:4])
    weights = [2.0 / (RELAX_SCALE * (diag_mid + nearby)) for nearby in diag_beside]
    diag_s = inv_sq * add_all(weights)
    return source, weights, diag_s, DAMPING * source / diag_s


def jacobi_sweep(padded, source, weights, diag_s, inv_sq):
    upd_mid, upd_beside = beside_all(padded)
    apply_s = inv_sq * add_all([weight * (upd_mid - nearby) for weight, nearby in zip(weights, upd_beside)])
    return upd_mid + DAMPING * (source - apply_s) / diag_s


def last_section(padded, relaxed, diag_a, velocity, pressure, inv_two):
    upd_mid, upd_beside = beside_all(padded)
    return velocity + relaxed - gradient(upd_beside, inv_two) / (RELAX_SCALE * diag_a), pressure + upd_mid


def run_level(state, force, pad_state, pad_corr, refresh, fixing, inv_sq, inv_two):
    relaxed, diag_a, resid_p = first_section(pad_state(state), force, inv_sq, inv_two)
    relaxed = fixing(relaxed)
    diag_a = fixing(diag_a)
    stacked = pad_corr(refresh(jnp.concatenate([relaxed, diag_a], 0)))
    planes = stacked.shape[1] - 2
    source, weights, diag_s, update = second_section(stacked, center(resid_p, planes), inv_sq, inv_two)
    update = fixing(update)
    for counter in range(SWEEPS - 1):
        padded = pad_corr(refresh(update))
        planes = padded.shape[1] - 2
        update = fixing(jacobi_sweep(padded, center(source, planes), [center(weight, planes) for weight in weights],
                                     center(diag_s, planes), inv_sq))
    padded = pad_corr(refresh(update))
    planes = padded.shape[1] - 2
    return last_section(padded, center(relaxed, planes), center(diag_a, planes), center(state[0:3], planes),
                      center(state[3:4], planes), inv_two)


def pad_flat(field_in):
    return jnp.pad(field_in, ((0, 0), (0, 0), (0, 0), (1, 1), (1, 1)))


def pad_planes(field_in):
    return jnp.pad(field_in, ((0, 0), (1, 1), (0, 0), (0, 0), (0, 0)))


def keep_same(field_in):
    return field_in


def link_tables(slot_spots, group_of, columns):
    spot_row = slot_spots[:, None]
    spot_col = slot_spots[None, :]
    usable = (spot_row >= 0) & (spot_col >= 0) & (group_of[:, None] == group_of[None, :])
    row_place = spot_row // columns
    col_place = spot_row % columns
    matches = [usable & (spot_col == spot_row - columns) & (row_place > 0),
               usable & (spot_col == spot_row + columns),
               usable & (spot_col == spot_row - 1) & (col_place > 0),
               usable & (spot_col == spot_row + 1) & (col_place < columns - 1)]
    tables = [matrix.astype(jnp.float32) for matrix in matches]
    return tables, [jnp.sum(matrix, axis=1) for matrix in tables]


def fetch_row(matrix, edge_rows):
    return jnp.einsum('jm,kwmx->kwjx', matrix, edge_rows, precision=PRECISE)


def side_pad(field_in, border, links):
    tables, counts_nb = links
    if border is None:
        border = jnp.zeros(field_in.shape[:3] + (field_in.shape[3] + 2, field_in.shape[4] + 2), field_in.dtype)
    row_low = jnp.where(counts_nb[0][:, None] > 0, fetch_row(tables[0], field_in[:, :, :, -1, :]), border[:, :, :, 0, 1:-1])
    row_high = jnp.where(counts_nb[1][:, None] > 0, fetch_row(tables[1], field_in[:, :, :, 0, :]), border[:, :, :, -1, 1:-1])
    middle = jnp.concatenate([row_low[:, :, :, None], field_in, row_high[:, :, :, None]], 3)
    col_low = jnp.where(counts_nb[2][:, None] > 0, fetch_row(tables[2], field_in[:, :, :, :, -1]), border[:, :, :, 1:-1, 0])
    col_high = jnp.where(counts_nb[3][:, None] > 0, fetch_row(tables[3], field_in[:, :, :, :, 0]), border[:, :, :, 1:-1, -1])
    col_low = jnp.concatenate([border[:, :, :, 0:1, 0], col_low, border[:, :, :, -1:, 0]], 3)
    col_high = jnp.concatenate([border[:, :, :, 0:1, -1], col_high, border[:, :, :, -1:, -1]], 3)
    return jnp.concatenate([col_low[..., None], middle, col_high[..., None]], 4)


def upsample(coarse_block):
    return jnp.repeat(jnp.repeat(jnp.repeat(coarse_block, 2, axis=1), 2, axis=2), 2, axis=3)


def coarsen(field_in):
    shaped = field_in.reshape(field_in.shape[0], field_in.shape[1] // 2, 2, field_in.shape[2],
                              field_in.shape[3] // 2, 2, field_in.shape[4] // 2, 2)
    return 0.125 * jnp.sum(shaped, axis=(2, 5, 7))


def reference(coarse_velocity, coarse_pressure, coarse_viscosity, coarse_force, refined_velocity_field, refined_pressure_field,
              refined_viscosity_field, refined_body_force, box_spots):
    coarse_state = jnp.concatenate([coarse_velocity, coarse_pressure[None], coarse_viscosity[None]], 0)[:, :, None]
    coarse_ext = pad_planes(coarse_state)
    coarse_vel_new, coarse_pres_new = run_level(coarse_ext, coarse_force[:, :, None], pad_flat, pad_flat,
                                                pad_planes, keep_same, 1.0, 0.5)
    group_of = (jnp.arange(box_spots.shape[0]) // FSLOT).astype(jnp.int32)
    links = link_tables(box_spots, group_of, XSPOTS)
    coarse_pad = jnp.pad(coarse_state[:, :, 0], ((0, 0), (1, 1), (1, 1), (1, 1)))
    half_z = FINE_CELLS_Z // 2
    half_y = FINE_CELLS_Y // 2
    half_x = FINE_CELLS_X // 2

    def inject_one(spot_no, group_no):
        spot_safe = jnp.maximum(spot_no, 0)
        start_z = (group_no * half_z).astype(jnp.int32)
        start_y = ((spot_safe // XSPOTS) * half_y).astype(jnp.int32)
        start_x = ((spot_safe % XSPOTS) * half_x).astype(jnp.int32)
        coarse_block = lax.dynamic_slice(coarse_pad, (jnp.int32(0), start_z, start_y, start_x),
                                         (5, half_z + 2, half_y + 2, half_x + 2))
        return upsample(coarse_block)[:, 1:-1, 1:-1, 1:-1]

    injection = jax.vmap(inject_one)(box_spots, group_of).transpose(1, 2, 0, 3, 4)
    fine_state = jnp.concatenate([refined_velocity_field, refined_pressure_field[None], refined_viscosity_field[None]], 0)
    inner_inj = injection[:, :, :, 1:-1, 1:-1]
    fine_ext = jnp.concatenate([inner_inj[:, 0:1], fine_state, inner_inj[:, -1:]], 1)
    fine_vel_new, fine_pres_new = run_level(fine_ext, refined_body_force, partial(side_pad, border=injection, links=links),
                                            partial(side_pad, border=None, links=links), pad_planes, keep_same,
                                            4.0, 1.0)
    occupied = (box_spots >= 0).astype(jnp.float32)[None, None, :, None, None]
    fine_vel_new = fine_vel_new * occupied
    fine_pres_new = fine_pres_new * occupied
    onehot = (box_spots[:, None] == jnp.arange(YSPOTS * XSPOTS, dtype=jnp.int32)[None, :]).astype(jnp.float32)
    onehot = onehot.reshape(N_BOXGRP, FSLOT, YSPOTS, XSPOTS)
    averaged = coarsen(jnp.concatenate([fine_vel_new, fine_pres_new], 0))
    grouped = averaged.reshape(4, half_z, N_BOXGRP, FSLOT, half_y, half_x)
    placed = jnp.einsum('kzgjyx,gjab->kgzaybx', grouped, onehot, precision=PRECISE).reshape(4, NZ, NY, NX)
    covered = jnp.repeat(jnp.repeat(jnp.sum(onehot, 1), half_y, 1), half_x, 2)
    covered = jnp.repeat(covered[:, None], half_z, 1).reshape(NZ, NY, NX)
    coarse_all = jnp.concatenate([coarse_vel_new, coarse_pres_new], 0)[:, :, 0]
    coarse_all = jnp.where(covered[None] > 0, placed, coarse_all)
    return coarse_all[0:3], coarse_all[3], fine_vel_new, fine_pres_new[0]
```

```python
import functools

import jax
import jax.numpy as jnp
from jax import lax
from jax.experimental import pallas as pl
from jax.experimental.pallas import tpu as pltpu
from jax.sharding import PartitionSpec as P

MESH = pl.DeviceIdType.MESH
F32 = jnp.float32
BF16 = jnp.bfloat16

HALF = 64
LANES = 128
TOP = 8

FN, FR = 8, 32
CN, CR = 4, 16

UZ, UR, UL, PR, MU, TZ, TR, DA, U1, U2 = range(10)
TL, RI, RV, VF = 0, 1, 2, 3


def lane_of(rows):
    return lax.broadcasted_iota(jnp.int32, (rows, LANES), 1)


def split3(x):
    hi = x.astype(BF16)
    rest = x - hi.astype(F32)
    mid = rest.astype(BF16)
    low = (rest - mid.astype(F32)).astype(BF16)
    return hi, mid, low


def pick_nt(sel, data):
    dims = (((1,), (1,)), ((), ()))
    return sum(
        lax.dot_general(sel, part, dims, preferred_element_type=F32) for part in split3(data)
    )


def pick_nn(data, sel):
    dims = (((1,), (0,)), ((), ()))
    return sum(
        lax.dot_general(part, sel, dims, preferred_element_type=F32) for part in split3(data)
    )


def one_where(cond):
    return jnp.where(cond, 1.0, 0.0).astype(BF16)


class Level:
    def __init__(self, planes, rows, inv_sq, inv_two, pad, flat):
        self.n, self.rows, self.inv_sq, self.inv_two = planes, rows, inv_sq, inv_two
        self.pad, self.flat = pad, flat
        lane = lane_of(rows) % HALF
        self.first = lane == 0
        self.last = lane == HALF - 1

    def mid(self, slot, z):
        return self.pad[slot, z, TOP : TOP + self.rows, :]

    def row_dn(self, slot, z):
        return self.pad[slot, z, TOP - 1 : TOP - 1 + self.rows, :]

    def row_up(self, slot, z):
        return self.pad[slot, z, TOP + 1 : TOP + 1 + self.rows, :]

    def lane_dn(self, x):
        return jnp.where(self.first, 0.0, pltpu.roll(x, 1, 1))

    def lane_up(self, x):
        return jnp.where(self.last, 0.0, pltpu.roll(x, LANES - 1, 1))

    def put(self, slot, z, x, ghost_lo=0.0, ghost_hi=0.0):
        self.pad[slot, z, TOP : TOP + self.rows, :] = x
        left = lane_of(1) < HALF
        head = pltpu.roll(x[0:1], HALF, 1)
        tail = pltpu.roll(x[self.rows - 1 : self.rows], HALF, 1)
        self.pad[slot, z, TOP - 1 : TOP, :] = jnp.where(left, ghost_lo, tail)
        self.pad[slot, z, TOP + self.rows : TOP + self.rows + 1, :] = jnp.where(
            left, head, ghost_hi
        )

    def around(self, slot, z):
        x = self.mid(slot, z)
        return x, [
            self.mid(slot, z - 1),
            self.mid(slot, z + 1),
            self.row_dn(slot, z),
            self.row_up(slot, z),
            self.lane_dn(x),
            self.lane_up(x),
        ]

    def relax(self, z, force):
        mu, nb = self.around(MU, z)
        sums = [mu + m for m in nb]
        total = (sums[0] + sums[1]) + (sums[2] + sums[3]) + (sums[4] + sums[5])
        half = 0.5 * self.inv_sq
        diag = (1.25 * half) * total
        inv = 1.0 / diag
        _, pres = self.around(PR, z)
        out = []
        for comp, slot in enumerate((UZ, UR, UL)):
            u, nb = self.around(slot, z)
            acc = functools.reduce(lambda a, b: a + b, [s * v for s, v in zip(sums, nb)])
            grad = self.inv_two * (pres[2 * comp + 1] - pres[2 * comp])
            out.append(0.2 * u + (force[comp] - grad + half * acc) * inv)
        self.pad[TZ, z, TOP : TOP + self.rows, :] = out[0]
        rows = self.rows
        self.put(
            TR,
            z,
            out[1],
            self.pad[UR, z, TOP - 1 : TOP, :],
            self.pad[UR, z, TOP + rows : TOP + rows + 1, :],
        )
        self.put(DA, z, diag)
        self.flat[TL, z] = out[2]
        self.flat[RI, z] = inv

    def first_update(self, z):
        tl = self.flat[TL, z]
        div = (
            (self.mid(TZ, z + 1) - self.mid(TZ, z - 1))
            + (self.row_up(TR, z) - self.row_dn(TR, z))
            + (self.lane_up(tl) - self.lane_dn(tl))
        )
        diag, nb = self.around(DA, z)
        faces = [1.0 / (diag + d) for d in nb]
        inv = 1.0 / ((faces[0] + faces[1]) + (faces[2] + faces[3]) + (faces[4] + faces[5]))
        for i, face in enumerate(faces):
            self.flat[VF + i, z] = face
        self.flat[RV, z] = inv
        self.put(U1, z, (-0.4 * self.inv_two / self.inv_sq) * div * inv)

    def sweep(self, z):
        u, nb = self.around(U1, z)
        acc = functools.reduce(
            lambda a, b: a + b, [self.flat[VF + i, z] * v for i, v in enumerate(nb)]
        )
        self.put(U2, z, 1.2 * u + (0.8 * self.flat[RV, z]) * acc)

    def finish(self, z):
        u, nb = self.around(U2, z)
        inv = self.inv_two * self.flat[RI, z]
        tees = (self.mid(TZ, z), self.mid(TR, z), self.flat[TL, z])
        vel = [t - (nb[2 * i + 1] - nb[2 * i]) * inv for i, t in enumerate(tees)]
        return vel, self.mid(PR, z) + u


def packed(raw, rows):
    return jnp.concatenate([raw[0:rows], raw[rows : 2 * rows]], axis=1)


def smooth_kernel(
    groups,
    subs,
    spots,
    cu_hbm,
    cp_hbm,
    cm_hbm,
    cf_hbm,
    fu_hbm,
    fp_hbm,
    fm_hbm,
    ff_hbm,
    fine_out,
    coarse_out,
    cu,
    cp,
    cm,
    cf,
    fu,
    fp,
    fm,
    ff,
    fpad,
    fflat,
    cpad,
    cflat,
    sb1,
    rb1,
    sb2,
    rb2,
    sb3,
    rb3,
    sb4,
    rb4,
    in_sem,
    send_sem,
    recv_sem,
):
    g = lax.axis_index("boxgrp")
    s = lax.axis_index("sub")
    up = (lax.rem(g + (s + 1) // subs, groups), lax.rem(s + 1, subs))
    down = (
        lax.rem(g + (groups - 1) + (s + subs - 1) // subs, groups),
        lax.rem(s + subs - 1, subs),
    )
    dev = g * subs + s
    at_low = dev == 0
    at_high = dev == groups * subs - 1
    box_low = s == 0
    box_high = s == subs - 1

    barrier = pltpu.get_barrier_semaphore()
    for neighbour in (up, down):
        pl.semaphore_signal(barrier, inc=1, device_id=neighbour, device_id_type=MESH)

    loads = []

    def load(src, dst):
        copy = pltpu.make_async_copy(src, dst, in_sem.at[len(loads)])
        copy.start()
        loads.append(copy)

    for src, dst in ((cu_hbm, cu), (cp_hbm, cp), (cm_hbm, cm)):
        load(src, dst)
    load(fu_hbm, fu)
    load(fp_hbm, fp)
    load(fm_hbm, fm)
    load(cf_hbm, cf)
    load(ff_hbm, ff)

    fine = Level(FN, FR, 4.0, 1.0, fpad, fflat)
    coarse = Level(CN, CR, 1.0, 0.5, cpad, cflat)

    for copy in loads[0:3]:
        copy.wait()

    def coarse_raw(slot, k):
        if slot == UZ:
            return cu[0, k]
        if slot == UR:
            return cu[2, k]
        if slot == UL:
            return cu[1, k]
        return cp[k] if slot == PR else cm[k]

    for k in range(CN):
        for slot in range(5):
            coarse.put(slot, k + 1, packed(coarse_raw(slot, k), CR))

    def for_fine(slot, k):
        if slot < PR:
            return cu[slot, k]
        return cp[k] if slot == PR else cm[k]

    edge = jnp.where(box_high, CN - 1, 0)
    q_edge = jnp.where(
        box_high, spots[lax.rem(g + 1, groups)], spots[lax.rem(g + groups - 1, groups)]
    )
    q_edge = jnp.maximum(q_edge, 0)
    row = lax.broadcasted_iota(jnp.int32, (2 * FR, HALF), 0)
    col = lax.broadcasted_iota(jnp.int32, (2 * FR, HALF), 1)
    pick_y = one_where(col == 32 * q_edge + row // 2)
    row = lax.broadcasted_iota(jnp.int32, (32, LANES), 0)
    col = lax.broadcasted_iota(jnp.int32, (32, LANES), 1)
    pick_x = one_where(row == (col % HALF) // 2)
    ghost = []
    for slot in range(5):
        plane = jnp.where(box_high, for_fine(slot, CN - 1), for_fine(slot, 0))
        ghost.append(pick_nt(pick_y, plane))
    ghost = pick_nn(jnp.concatenate(ghost, axis=0), pick_x)
    left = lane_of(FR) < HALF
    ghost = [
        jnp.where(left, ghost[64 * i : 64 * i + 32], ghost[64 * i + 32 : 64 * i + 64])
        for i in range(5)
    ]

    q_own = spots[g]
    col = lax.broadcasted_iota(jnp.int32, (16, HALF), 1)
    pick_row = one_where(col == jnp.where(q_own == 1, 31, 32))
    rows = []
    for slot in range(5):
        planes = jnp.concatenate([for_fine(slot, k) for k in range(CN)], axis=0)
        rows.append(pick_nt(pick_row, planes))
    row = lax.broadcasted_iota(jnp.int32, (LANES, CN * LANES), 0)
    col = lax.broadcasted_iota(jnp.int32, (LANES, CN * LANES), 1)
    pick_k = one_where(row == 32 * (col // LANES) + (col % HALF) // 2)
    rows = pick_nn(jnp.concatenate(rows, axis=0), pick_k)

    def fine_raw(slot, z):
        if slot < PR:
            return fu[slot, z]
        return fp[z] if slot == PR else fm[z]

    for copy in loads[3:6]:
        copy.wait()
    for z in range(FN):
        for slot in range(5):
            k = z // 2
            line = rows[16 * slot : 16 * slot + 1, LANES * k : LANES * (k + 1)]
            lo = jnp.where(q_own == 1, line, 0.0)
            hi = jnp.where(q_own == 1, 0.0, line)
            fine.put(slot, z + 1, packed(fine_raw(slot, z), FR), lo, hi)

    for slot in range(5):
        at = slice(slot * FR, (slot + 1) * FR)
        sb1[0, at, :] = jnp.where(box_high, ghost[slot], fine.mid(slot, FN))
        sb1[1, at, :] = jnp.where(box_low, ghost[slot], fine.mid(slot, 1))
        at = slice(5 * FR + slot * CR, 5 * FR + (slot + 1) * CR)
        sb1[0, at, :] = coarse.mid(slot, CN)
        sb1[1, at, :] = coarse.mid(slot, 1)

    sends = []

    def exchange(sb, rb):
        pair = []
        for side, device in enumerate((up, down)):
            i = len(sends)
            copy = pltpu.make_async_remote_copy(
                src_ref=sb.at[side],
                dst_ref=rb.at[side],
                send_sem=send_sem.at[i],
                recv_sem=recv_sem.at[i],
                device_id=device,
                device_id_type=MESH,
            )
            copy.start()
            sends.append(copy)
            pair.append(copy)
        return pair

    def arrive(pair):
        for copy in pair:
            copy.wait_recv()

    def both(fine_step, coarse_step):
        @pl.loop(2, FN)
        def _(z):
            fine_step(z)

        @pl.loop(2, CN)
        def _(z):
            coarse_step(z)

    def ends(fine_step, coarse_step):
        for z in (1, FN):
            fine_step(z)
        for z in (1, CN):
            coarse_step(z)

    def fine_relax(z):
        fine.relax(z, [packed(ff[c, z - 1], FR) for c in range(3)])

    def coarse_relax(z):
        coarse.relax(z, [packed(cf[c, z - 1], CR) for c in (0, 2, 1)])

    pl.semaphore_wait(barrier, 2)
    pair = exchange(sb1, rb1)
    for copy in loads[6:8]:
        copy.wait()
    both(fine_relax, coarse_relax)
    arrive(pair)
    for slot in range(5):
        for side, out_side, z in ((0, at_low, 0), (1, at_high, FN + 1)):
            value = rb1[side, slot * FR : (slot + 1) * FR, :]
            fpad[slot, z, TOP : TOP + FR, :] = jnp.where(out_side, 0.0, value)
        for side, out_side, z in ((0, at_low, 0), (1, at_high, CN + 1)):
            value = rb1[side, 5 * FR + slot * CR : 5 * FR + (slot + 1) * CR, :]
            cpad[slot, z, TOP : TOP + CR, :] = jnp.where(out_side, 0.0, value)
    ends(fine_relax, coarse_relax)

    for side, zf, zc in ((0, FN, CN), (1, 1, 1)):
        sb2[side, 0:32, :] = fine.mid(TZ, zf)
        sb2[side, 32:64, :] = fine.mid(DA, zf)
        sb2[side, 64:80, :] = coarse.mid(TZ, zc)
        sb2[side, 80:96, :] = coarse.mid(DA, zc)
    pair = exchange(sb2, rb2)
    both(fine.first_update, coarse.first_update)
    arrive(pair)
    for side, box_side, out_side, zf, zc in (
        (0, box_low, at_low, 0, 0),
        (1, box_high, at_high, FN + 1, CN + 1),
    ):
        at = slice(TOP, TOP + FR)
        fpad[TZ, zf, at, :] = jnp.where(box_side, fpad[UZ, zf, at, :], rb2[side, 0:32, :])
        fpad[DA, zf, at, :] = jnp.where(box_side, 0.0, rb2[side, 32:64, :])
        at = slice(TOP, TOP + CR)
        cpad[TZ, zc, at, :] = jnp.where(out_side, 0.0, rb2[side, 64:80, :])
        cpad[DA, zc, at, :] = jnp.where(out_side, 0.0, rb2[side, 80:96, :])
    ends(fine.first_update, coarse.first_update)

    def swap_update(slot, sb, rb, fine_step, coarse_step):
        for side, zf, zc in ((0, FN, CN), (1, 1, 1)):
            sb[side, 0:32, :] = fine.mid(slot, zf)
            sb[side, 32:48, :] = coarse.mid(slot, zc)
        pair = exchange(sb, rb)
        both(fine_step, coarse_step)
        arrive(pair)
        for side, box_side, out_side, zf, zc in (
            (0, box_low, at_low, 0, 0),
            (1, box_high, at_high, FN + 1, CN + 1),
        ):
            fpad[slot, zf, TOP : TOP + FR, :] = jnp.where(box_side, 0.0, rb[side, 0:32, :])
            cpad[slot, zc, TOP : TOP + CR, :] = jnp.where(out_side, 0.0, rb[side, 32:48, :])
        ends(fine_step, coarse_step)

    def fine_finish(z):
        vel, pres = fine.finish(z)
        for i in range(3):
            fine_out[i, z - 1] = vel[i]
        fine_out[3, z - 1] = pres

    def coarse_finish(z):
        vel, pres = coarse.finish(z)
        for i, c in enumerate((0, 2, 1)):
            coarse_out[c, z - 1] = vel[i]
        coarse_out[3, z - 1] = pres

    swap_update(U1, sb3, rb3, fine.sweep, coarse.sweep)
    swap_update(U2, sb4, rb4, fine_finish, coarse_finish)
    for copy in sends:
        copy.wait_send()


def place_kernel(spots, fine_in, coarse_in, fvel, fpres, cvel, cpres):
    q = spots[lax.axis_index("boxgrp")]
    filled = q >= 0
    dims = (((1,), (1,)), ((), ()))
    pairs = []
    for f in range(4):
        for k in range(CN):
            for z in (2 * k, 2 * k + 1):
                x = jnp.where(filled, fine_in[f, z], 0.0)
                for half in range(2):
                    piece = x[:, half * HALF : (half + 1) * HALF]
                    at = slice(half * FR, (half + 1) * FR)
                    if f < 3:
                        fvel[f, z, at, :] = piece
                    else:
                        fpres[z, at, :] = piece
            ref = fvel.at[f] if f < 3 else fpres
            total = None
            for z in (2 * k, 2 * k + 1):
                for start in range(2):
                    part = ref[z, pl.ds(start, FR, stride=2), :]
                    total = part if total is None else total + part
            pairs.append(total)
    row = lax.broadcasted_iota(jnp.int32, (32, HALF), 0)
    col = lax.broadcasted_iota(jnp.int32, (32, HALF), 1)
    mean = jnp.where(row == col // 2, 0.125, 0.0).astype(BF16)
    lane = lane_of(32)
    for f in range(4):
        blk = pick_nt(mean, jnp.concatenate(pairs[4 * f : 4 * f + 4], axis=0))
        for k in range(CN):
            lo = pltpu.roll(blk, (LANES - 32 * k) % LANES, 1) if k else blk
            hi = pltpu.roll(blk, (LANES + 32 - 32 * k) % LANES, 1) if k != 1 else blk
            covered = jnp.where(lane < 32, lo, hi)[:, 0:HALF]
            x = coarse_in[f, k]
            own = jnp.concatenate([x[:, 0:HALF], x[:, HALF:LANES]], axis=0)
            value = jnp.where(lane[:, 0:HALF] // 32 == q, covered, own)
            if f < 3:
                cvel[f, k] = value
            else:
                cpres[k] = value


def on_device(groups, subs, cu, cp, cm, cf, fu, fp, fm, ff, spots):
    cu, cf = [a.transpose(0, 1, 3, 2) for a in (cu, cf)]
    cp, cm = [a.transpose(0, 2, 1) for a in (cp, cm)]
    fu, ff = [a[:, :, 0] for a in (fu, ff)]
    fp, fm = [a[:, 0] for a in (fp, fm)]
    vmem = functools.partial(pltpu.VMEM, dtype=F32)
    smem_spec = pl.BlockSpec(memory_space=pltpu.SMEM)
    any_spec = pl.BlockSpec(memory_space=pl.ANY)
    vmem_spec = pl.BlockSpec(memory_space=pltpu.VMEM)
    fine, coarse = pl.pallas_call(
        functools.partial(smooth_kernel, groups, subs),
        out_shape=(
            jax.ShapeDtypeStruct((4, FN, FR, LANES), F32),
            jax.ShapeDtypeStruct((4, CN, CR, LANES), F32),
        ),
        in_specs=[smem_spec] + [any_spec] * 8,
        out_specs=(vmem_spec, vmem_spec),
        scratch_shapes=[vmem(a.shape) for a in (cu, cp, cm, cf, fu, fp, fm, ff)]
        + [
            vmem((10, FN + 2, FR + 16, LANES)),
            vmem((9, FN + 2, FR, LANES)),
            vmem((10, CN + 2, CR + 16, LANES)),
            vmem((9, CN + 2, CR, LANES)),
        ]
        + [vmem((2, r * (FR + CR), LANES)) for r in (5, 5, 2, 2, 1, 1, 1, 1)]
        + [
            pltpu.SemaphoreType.DMA((8,)),
            pltpu.SemaphoreType.DMA((8,)),
            pltpu.SemaphoreType.DMA((8,)),
        ],
        compiler_params=pltpu.CompilerParams(
            collective_id=0, has_side_effects=True, vmem_limit_bytes=32 * 1024 * 1024
        ),
        name="smooth",
    )(spots, cu, cp, cm, cf, fu, fp, fm, ff)
    fvel, fpres, cvel, cpres = pl.pallas_call(
        place_kernel,
        out_shape=tuple(jax.ShapeDtypeStruct(a.shape, F32) for a in (fu, fp, cu, cp)),
        in_specs=[smem_spec, vmem_spec, vmem_spec],
        out_specs=(vmem_spec,) * 4,
        compiler_params=pltpu.CompilerParams(vmem_limit_bytes=16 * 1024 * 1024),
        name="place",
    )(spots, fine, coarse)
    return (
        cvel.transpose(0, 1, 3, 2),
        cpres.transpose(0, 2, 1),
        fvel[:, :, None],
        fpres[:, None],
    )


def solution(mesh):
    groups, subs = mesh.shape["boxgrp"], mesh.shape["sub"]
    zs = ("boxgrp", "sub")
    return jax.shard_map(
        functools.partial(on_device, groups, subs),
        mesh=mesh,
        in_specs=(
            P(None, zs, None, None),
            P(zs, None, None),
            P(zs, None, None),
            P(None, zs, None, None),
            P(None, "sub", "boxgrp", None, None),
            P("sub", "boxgrp", None, None),
            P("sub", "boxgrp", None, None),
            P(None, "sub", "boxgrp", None, None),
            P(),
        ),
        out_specs=(
            P(None, zs, None, None),
            P(zs, None, None),
            P(None, "sub", "boxgrp", None, None),
            P("sub", "boxgrp", None, None),
        ),
        check_vma=False,
    )
```

```python
import functools

import jax
import jax.numpy as jnp
from jax import lax
from jax.experimental import pallas as pl
from jax.experimental.pallas import tpu as pltpu
from jax.sharding import PartitionSpec as P

MESH = pl.DeviceIdType.MESH
F32 = jnp.float32
BF16 = jnp.bfloat16

HALF = 64
LANES = 128
TOP = 8

FN, FR = 8, 32
CN, CR = 4, 16

OFF = 4
DEEP = 4

UZ, UR, UL, PR, MU, TZ, TR, DA, U1, U2 = range(10)
TL, RI, RV, S0, F0, F1, F2, VF = 0, 1, 2, 3, 4, 5, 6, 7
FLAT = VF + 6

COARSE_MSG = (
    (UZ, True, 4),
    (PR, True, 4),
    (MU, True, 4),
    (UR, True, 3),
    (UL, True, 3),
    (F0, False, 3),
    (F1, False, 2),
    (F2, False, 2),
)
COARSE_ROWS = CR * sum(depth for _, _, depth in COARSE_MSG)


def lane_of(rows):
    return lax.broadcasted_iota(jnp.int32, (rows, LANES), 1)


def split3(x):
    hi = x.astype(BF16)
    rest = x - hi.astype(F32)
    mid = rest.astype(BF16)
    low = (rest - mid.astype(F32)).astype(BF16)
    return hi, mid, low


def pick_nt(sel, data):
    dims = (((1,), (1,)), ((), ()))
    return sum(
        lax.dot_general(sel, part, dims, preferred_element_type=F32) for part in split3(data)
    )


def pick_nn(data, sel):
    dims = (((1,), (0,)), ((), ()))
    return sum(
        lax.dot_general(part, sel, dims, preferred_element_type=F32) for part in split3(data)
    )


def one_where(cond):
    return jnp.where(cond, 1.0, 0.0).astype(BF16)


class Level:
    def __init__(self, planes, rows, inv_sq, inv_two, pad, flat):
        self.n, self.rows, self.inv_sq, self.inv_two = planes, rows, inv_sq, inv_two
        self.pad, self.flat = pad, flat
        lane = lane_of(rows) % HALF
        self.first = lane == 0
        self.last = lane == HALF - 1

    def mid(self, slot, z):
        return self.pad[slot, z + OFF, TOP : TOP + self.rows, :]

    def row_dn(self, slot, z):
        return self.pad[slot, z + OFF, TOP - 1 : TOP - 1 + self.rows, :]

    def row_up(self, slot, z):
        return self.pad[slot, z + OFF, TOP + 1 : TOP + 1 + self.rows, :]

    def lane_dn(self, x):
        return jnp.where(self.first, 0.0, pltpu.roll(x, 1, 1))

    def lane_up(self, x):
        return jnp.where(self.last, 0.0, pltpu.roll(x, LANES - 1, 1))

    def get(self, slot, z):
        return self.flat[slot, z + OFF]

    def keep(self, slot, z, x):
        self.flat[slot, z + OFF] = x

    def set_mid(self, slot, z, x):
        self.pad[slot, z + OFF, TOP : TOP + self.rows, :] = x

    def put(self, slot, z, x, ghost_lo=0.0, ghost_hi=0.0):
        self.set_mid(slot, z, x)
        left = lane_of(1) < HALF
        head = pltpu.roll(x[0:1], HALF, 1)
        tail = pltpu.roll(x[self.rows - 1 : self.rows], HALF, 1)
        self.pad[slot, z + OFF, TOP - 1 : TOP, :] = jnp.where(left, ghost_lo, tail)
        self.pad[slot, z + OFF, TOP + self.rows : TOP + self.rows + 1, :] = jnp.where(
            left, head, ghost_hi
        )

    def around(self, slot, z):
        x = self.mid(slot, z)
        return x, [
            self.mid(slot, z - 1),
            self.mid(slot, z + 1),
            self.row_dn(slot, z),
            self.row_up(slot, z),
            self.lane_dn(x),
            self.lane_up(x),
        ]

    def relax(self, z, full=True, drop=None):
        def kept(x):
            return x if drop is None else jnp.where(drop, 0.0, x)

        mu, nb = self.around(MU, z)
        sums = [mu + m for m in nb]
        total = (sums[0] + sums[1]) + (sums[2] + sums[3]) + (sums[4] + sums[5])
        half = 0.5 * self.inv_sq
        diag = (1.25 * half) * total
        inv = 1.0 / diag
        _, pres = self.around(PR, z)
        out = []
        for comp, slot in enumerate((UZ, UR, UL) if full else (UZ,)):
            u, nb = self.around(slot, z)
            prod = [s * v for s, v in zip(sums, nb)]
            acc = (prod[0] + prod[1]) + (prod[2] + prod[3]) + (prod[4] + prod[5])
            grad = self.inv_two * (pres[2 * comp + 1] - pres[2 * comp])
            out.append(0.2 * u + (self.get(F0 + comp, z) - grad + half * acc) * inv)
        self.set_mid(TZ, z, kept(out[0]))
        self.put(DA, z, kept(diag))
        self.keep(RI, z, inv)
        if full:
            end = TOP + self.rows
            self.put(
                TR,
                z,
                out[1],
                self.pad[UR, z + OFF, TOP - 1 : TOP, :],
                self.pad[UR, z + OFF, end : end + 1, :],
            )
            self.keep(TL, z, out[2])
            self.keep(
                S0,
                z,
                (self.row_up(TR, z) - self.row_dn(TR, z))
                + (self.lane_up(out[2]) - self.lane_dn(out[2])),
            )

    def first_update(self, z, drop=None):
        div = (self.mid(TZ, z + 1) - self.mid(TZ, z - 1)) + self.get(S0, z)
        diag, nb = self.around(DA, z)
        faces = [1.0 / (diag + d) for d in nb]
        inv = 1.0 / ((faces[0] + faces[1]) + (faces[2] + faces[3]) + (faces[4] + faces[5]))
        for i, face in enumerate(faces):
            self.keep(VF + i, z, face)
        self.keep(RV, z, inv)
        value = (-0.4 * self.inv_two / self.inv_sq) * div * inv
        self.put(U1, z, value if drop is None else jnp.where(drop, 0.0, value))

    def sweep(self, z, drop=None):
        u, nb = self.around(U1, z)
        prod = [self.get(VF + i, z) * v for i, v in enumerate(nb)]
        acc = (prod[0] + prod[1]) + (prod[2] + prod[3]) + (prod[4] + prod[5])
        value = 1.2 * u + (0.8 * self.get(RV, z)) * acc
        self.put(U2, z, value if drop is None else jnp.where(drop, 0.0, value))

    def finish(self, z):
        u, nb = self.around(U2, z)
        inv = self.inv_two * self.get(RI, z)
        tees = (self.mid(TZ, z), self.mid(TR, z), self.get(TL, z))
        vel = [t - (nb[2 * i + 1] - nb[2 * i]) * inv for i, t in enumerate(tees)]
        return vel, self.mid(PR, z) + u


def packed(raw, rows):
    return jnp.concatenate([raw[0:rows], raw[rows : 2 * rows]], axis=1)


def smooth_kernel(
    groups,
    subs,
    spots,
    cu_hbm,
    cp_hbm,
    cm_hbm,
    cf_hbm,
    fu_hbm,
    fp_hbm,
    fm_hbm,
    ff_hbm,
    fine_hbm,
    coarse_hbm,
    cu,
    cp,
    cm,
    cf,
    fu,
    fp,
    fm,
    ff,
    fpad,
    fflat,
    cpad,
    cflat,
    fine_out,
    coarse_out,
    sb1,
    rb1,
    sbc,
    rbc,
    sb2,
    rb2,
    in_sem,
    out_sem,
    send1,
    recv1,
    sendc,
    recvc,
    send2,
    recv2,
):
    g = lax.axis_index("boxgrp")
    s = lax.axis_index("sub")
    up_g, up_s = lax.rem(g + (s + 1) // subs, groups), lax.rem(s + 1, subs)
    down_g = lax.rem(g + (groups - 1) + (s + subs - 1) // subs, groups)
    down_s = lax.rem(s + subs - 1, subs)
    dev = g * subs + s
    has_up = dev < groups * subs - 1
    has_down = dev > 0
    box_low = s == 0
    box_high = s == subs - 1

    barrier = pltpu.get_barrier_semaphore()

    @pl.when(has_up)
    def _():
        pl.semaphore_signal(barrier, inc=1, device_id=(up_g, up_s), device_id_type=MESH)

    @pl.when(has_down)
    def _():
        pl.semaphore_signal(barrier, inc=1, device_id=(down_g, down_s), device_id_type=MESH)

    loads = []

    def load(src, dst):
        copy = pltpu.make_async_copy(src, dst, in_sem.at[len(loads)])
        copy.start()
        loads.append(copy)

    for z in (0, FN - 1):
        load(fu_hbm.at[:, z], fu.at[:, z])
        load(fp_hbm.at[z], fp.at[z])
        load(fm_hbm.at[z], fm.at[z])
    for src, dst in ((cu_hbm, cu), (cp_hbm, cp), (cm_hbm, cm), (cf_hbm, cf)):
        load(src, dst)
    inner = pl.ds(1, FN - 2)
    load(fu_hbm.at[:, inner], fu.at[:, inner])
    load(fp_hbm.at[inner], fp.at[inner])
    load(fm_hbm.at[inner], fm.at[inner])
    load(ff_hbm, ff)

    fine = Level(FN, FR, 4.0, 1.0, fpad, fflat)
    coarse = Level(CN, CR, 1.0, 0.5, cpad, cflat)

    def fine_raw(slot, z):
        if slot < PR:
            return fu[slot, z]
        return fp[z] if slot == PR else fm[z]

    def coarse_raw(slot, k):
        if slot in (UZ, UR, UL):
            return cu[(0, 2, 1)[slot], k]
        return cp[k] if slot == PR else cm[k]

    def for_fine(slot, k):
        if slot < PR:
            return cu[slot, k]
        return cp[k] if slot == PR else cm[k]

    def remote(sb, rb, send, recv, side):
        return pltpu.make_async_remote_copy(
            src_ref=sb.at[side],
            dst_ref=rb.at[side],
            send_sem=send.at[side],
            recv_sem=recv.at[side],
            device_id=(
                jnp.where(side == 0, up_g, down_g),
                jnp.where(side == 0, up_s, down_s),
            ),
            device_id_type=MESH,
        )

    for copy in loads[0:6]:
        copy.wait()
    for slot in range(5):
        at = slice(slot * FR, (slot + 1) * FR)
        sb1[0, at, :] = packed(fine_raw(slot, FN - 1), FR)
        sb1[1, at, :] = packed(fine_raw(slot, 0), FR)

    @pl.when(has_up & has_down)
    def _():
        pl.semaphore_wait(barrier, 2)

    @pl.when(~(has_up & has_down))
    def _():
        pl.semaphore_wait(barrier, 1)

    one_up = remote(sb1, rb1, send1, recv1, 0)
    one_down = remote(sb1, rb1, send1, recv1, 1)
    pl.when(s < subs - 1)(one_up.start)
    pl.when(s > 0)(one_down.start)

    for copy in loads[6:10]:
        copy.wait()

    @pl.when(box_low | box_high)
    def _():
        q_edge = jnp.where(
            box_high, spots[lax.rem(g + 1, groups)], spots[lax.rem(g + groups - 1, groups)]
        )
        q_edge = jnp.maximum(q_edge, 0)
        row = lax.broadcasted_iota(jnp.int32, (2 * FR, HALF), 0)
        col = lax.broadcasted_iota(jnp.int32, (2 * FR, HALF), 1)
        pick_y = one_where(col == 32 * q_edge + row // 2)
        row = lax.broadcasted_iota(jnp.int32, (32, LANES), 0)
        col = lax.broadcasted_iota(jnp.int32, (32, LANES), 1)
        pick_x = one_where(row == (col % HALF) // 2)
        ghost = []
        for slot in range(5):
            plane = jnp.where(box_high, for_fine(slot, CN - 1), for_fine(slot, 0))
            ghost.append(pick_nt(pick_y, plane))
        ghost = pick_nn(jnp.concatenate(ghost, axis=0), pick_x)
        left = lane_of(FR) < HALF
        side = jnp.where(box_high, 0, 1)
        for i in range(5):
            sb1[side, i * FR : (i + 1) * FR, :] = jnp.where(
                left, ghost[64 * i : 64 * i + 32], ghost[64 * i + 32 : 64 * i + 64]
            )

    pl.when(box_high & has_up)(one_up.start)
    pl.when(box_low & has_down)(one_down.start)

    for k in range(CN):
        for slot in range(5):
            coarse.put(slot, k, packed(coarse_raw(slot, k), CR))
        for comp in range(3):
            coarse.keep(F0 + comp, k, packed(cf[(0, 2, 1)[comp], k], CR))
    base = 0
    for slot, padded, depth in COARSE_MSG:
        read = coarse.mid if padded else coarse.get
        for d in range(depth):
            sbc[0, base : base + CR, :] = read(slot, CN - 1 - d)
            sbc[1, base : base + CR, :] = read(slot, d)
            base += CR
    deep_up = remote(sbc, rbc, sendc, recvc, 0)
    deep_down = remote(sbc, rbc, sendc, recvc, 1)
    pl.when(has_up)(deep_up.start)
    pl.when(has_down)(deep_down.start)

    q_own = spots[g]
    col = lax.broadcasted_iota(jnp.int32, (16, HALF), 1)
    pick_row = one_where(col == jnp.where(q_own == 1, 31, 32))
    rows = []
    for slot in range(5):
        planes = jnp.concatenate([for_fine(slot, k) for k in range(CN)], axis=0)
        rows.append(pick_nt(pick_row, planes))
    row = lax.broadcasted_iota(jnp.int32, (LANES, CN * LANES), 0)
    col = lax.broadcasted_iota(jnp.int32, (LANES, CN * LANES), 1)
    pick_k = one_where(row == 32 * (col // LANES) + (col % HALF) // 2)
    rows = pick_nn(jnp.concatenate(rows, axis=0), pick_k)

    for copy in loads[10:14]:
        copy.wait()
    for z in range(FN):
        for slot in range(5):
            k = z // 2
            line = rows[16 * slot : 16 * slot + 1, LANES * k : LANES * (k + 1)]
            lo = jnp.where(q_own == 1, line, 0.0)
            hi = jnp.where(q_own == 1, 0.0, line)
            fine.put(slot, z, packed(fine_raw(slot, z), FR), lo, hi)
        for comp in range(3):
            fine.keep(F0 + comp, z, packed(ff[comp, z], FR))

    @pl.loop(1, FN - 1)
    def _(z):
        fine.relax(z)

    @pl.loop(0, 2)
    def _(step):
        side = jnp.where(s < subs // 2, 1 - step, step)
        low = side == 0
        there = (low & has_down) | ((side == 1) & has_up)
        pl.when(there)(remote(sb1, rb1, send1, recv1, side).wait_recv)
        edge = jnp.where(low, 0, FN - 1)
        beyond = jnp.where(low, -1, FN)
        for slot in range(5):
            value = rb1[side, slot * FR : (slot + 1) * FR, :]
            fine.set_mid(slot, beyond, jnp.where(there, value, 0.0))
        fine.relax(edge)
        inward = jnp.where(low, 1, -1)
        back = 1 - side
        for d in range(3):
            sb2[back, d * FR : (d + 1) * FR, :] = fine.mid(TZ, edge + inward * d)
            sb2[back, (3 + d) * FR : (4 + d) * FR, :] = fine.mid(DA, edge + inward * d)
        for d in range(2):
            sb2[back, (6 + d) * FR : (7 + d) * FR, :] = fine.get(S0, edge + inward * d)
        same_box = (low & (s > 0)) | ((side == 1) & (s < subs - 1))
        pl.when(same_box)(remote(sb2, rb2, send2, recv2, back).start)

    outs = []

    def store(src, dst):
        copy = pltpu.make_async_copy(src, dst, out_sem.at[len(outs)])
        copy.start()
        outs.append(copy)

    def fine_finish(z):
        vel, pres = fine.finish(z)
        for i in range(3):
            fine_out[i, z] = vel[i]
        fine_out[3, z] = pres

    @pl.loop(1, FN - 1)
    def _(z):
        fine.first_update(z)

    @pl.loop(2, FN - 2)
    def _(z):
        fine.sweep(z)

    @pl.loop(3, FN - 3)
    def _(z):
        fine_finish(z)

    pl.when(has_down)(deep_up.wait_recv)
    pl.when(has_up)(deep_down.wait_recv)
    base = 0
    for slot, padded, depth in COARSE_MSG:
        write = coarse.put if padded else coarse.keep
        for d in range(depth):
            at = slice(base, base + CR)
            write(slot, -1 - d, jnp.where(has_down, rbc[0, at, :], 0.0))
            write(slot, CN + d, jnp.where(has_up, rbc[1, at, :], 0.0))
            base += CR
    no_down, no_up = dev == 0, dev == groups * subs - 1
    coarse.relax(-3, False, no_down)
    coarse.relax(CN + 2, False, no_up)
    for d in (2, 1):
        coarse.relax(-d, True, no_down)
        coarse.relax(CN - 1 + d, True, no_up)
    for z in range(CN):
        coarse.relax(z)
    for d in (2, 1):
        coarse.first_update(-d, no_down)
        coarse.first_update(CN - 1 + d, no_up)
    for z in range(CN):
        coarse.first_update(z)
    coarse.sweep(-1, no_down)
    coarse.sweep(CN, no_up)
    for z in range(CN):
        coarse.sweep(z)
    for z in range(CN):
        vel, pres = coarse.finish(z)
        for i, c in enumerate((0, 2, 1)):
            coarse_out[c, z] = vel[i]
        coarse_out[3, z] = pres
    store(coarse_out, coarse_hbm)
    store(fine_out.at[:, pl.ds(3, FN - 6)], fine_hbm.at[:, pl.ds(3, FN - 6)])

    pl.when(s > 0)(remote(sb2, rb2, send2, recv2, 0).wait_recv)
    pl.when(s < subs - 1)(remote(sb2, rb2, send2, recv2, 1).wait_recv)
    for side, end, beyond, way in ((0, box_low, -1, -1), (1, box_high, FN, 1)):
        for d in range(3):
            z = beyond + way * d
            tz = rb2[side, d * FR : (d + 1) * FR, :]
            fine.set_mid(TZ, z, jnp.where(end, fine.mid(UZ, beyond), tz))
            diag = rb2[side, (3 + d) * FR : (4 + d) * FR, :]
            fine.put(DA, z, jnp.where(end, 0.0, diag))
            if d < 2:
                fine.keep(S0, z, rb2[side, (6 + d) * FR : (7 + d) * FR, :])
    fine.first_update(0)
    fine.first_update(FN - 1)
    for d in (1, 2):
        fine.first_update(-d, box_low)
        fine.first_update(FN - 1 + d, box_high)
    fine.sweep(-1, box_low)
    fine.sweep(FN, box_high)
    for z in (0, 1, FN - 2, FN - 1):
        fine.sweep(z)
    for z in (0, 1, 2):
        fine_finish(z)
    store(fine_out.at[:, pl.ds(0, 3)], fine_hbm.at[:, pl.ds(0, 3)])
    for z in (FN - 3, FN - 2, FN - 1):
        fine_finish(z)
    store(fine_out.at[:, pl.ds(FN - 3, 3)], fine_hbm.at[:, pl.ds(FN - 3, 3)])

    pl.when(has_up)(one_up.wait_send)
    pl.when(has_down)(one_down.wait_send)
    pl.when(has_up)(deep_up.wait_send)
    pl.when(has_down)(deep_down.wait_send)
    pl.when(s < subs - 1)(remote(sb2, rb2, send2, recv2, 0).wait_send)
    pl.when(s > 0)(remote(sb2, rb2, send2, recv2, 1).wait_send)
    for copy in outs:
        copy.wait()


def place_kernel(spots, fine_in, coarse_in, fvel, fpres, cvel, cpres):
    q = spots[lax.axis_index("boxgrp")]
    filled = q >= 0
    dims = (((1,), (1,)), ((), ()))
    pairs = []
    for f in range(4):
        for k in range(CN):
            for z in (2 * k, 2 * k + 1):
                x = jnp.where(filled, fine_in[f, z], 0.0)
                for half in range(2):
                    piece = x[:, half * HALF : (half + 1) * HALF]
                    at = slice(half * FR, (half + 1) * FR)
                    if f < 3:
                        fvel[f, z, at, :] = piece
                    else:
                        fpres[z, at, :] = piece
            ref = fvel.at[f] if f < 3 else fpres
            total = None
            for z in (2 * k, 2 * k + 1):
                for start in range(2):
                    part = ref[z, pl.ds(start, FR, stride=2), :]
                    total = part if total is None else total + part
            pairs.append(total)
    row = lax.broadcasted_iota(jnp.int32, (32, HALF), 0)
    col = lax.broadcasted_iota(jnp.int32, (32, HALF), 1)
    mean = jnp.where(row == col // 2, 0.125, 0.0).astype(BF16)
    lane = lane_of(32)
    for f in range(4):
        blk = pick_nt(mean, jnp.concatenate(pairs[4 * f : 4 * f + 4], axis=0))
        for k in range(CN):
            lo = pltpu.roll(blk, (LANES - 32 * k) % LANES, 1) if k else blk
            hi = pltpu.roll(blk, (LANES + 32 - 32 * k) % LANES, 1) if k != 1 else blk
            covered = jnp.where(lane < 32, lo, hi)[:, 0:HALF]
            x = coarse_in[f, k]
            own = jnp.concatenate([x[:, 0:HALF], x[:, HALF:LANES]], axis=0)
            value = jnp.where(lane[:, 0:HALF] // 32 == q, covered, own)
            if f < 3:
                cvel[f, k] = value
            else:
                cpres[k] = value


def on_device(groups, subs, cu, cp, cm, cf, fu, fp, fm, ff, spots):
    cu, cf = [a.transpose(0, 1, 3, 2) for a in (cu, cf)]
    cp, cm = [a.transpose(0, 2, 1) for a in (cp, cm)]
    fu, ff = [a[:, :, 0] for a in (fu, ff)]
    fp, fm = [a[:, 0] for a in (fp, fm)]
    vmem = functools.partial(pltpu.VMEM, dtype=F32)
    smem_spec = pl.BlockSpec(memory_space=pltpu.SMEM)
    hbm_spec = pl.BlockSpec(memory_space=pltpu.HBM)
    vmem_spec = pl.BlockSpec(memory_space=pltpu.VMEM)
    fine, coarse = pl.pallas_call(
        functools.partial(smooth_kernel, groups, subs),
        out_shape=(
            jax.ShapeDtypeStruct((4, FN, FR, LANES), F32),
            jax.ShapeDtypeStruct((4, CN, CR, LANES), F32),
        ),
        in_specs=[smem_spec] + [hbm_spec] * 8,
        out_specs=(hbm_spec, hbm_spec),
        scratch_shapes=[vmem(a.shape) for a in (cu, cp, cm, cf, fu, fp, fm, ff)]
        + [
            vmem((10, FN + 2 * OFF, FR + 16, LANES)),
            vmem((FLAT, FN + 2 * OFF, FR, LANES)),
            vmem((10, CN + 2 * OFF, CR + 16, LANES)),
            vmem((FLAT, CN + 2 * OFF, CR, LANES)),
            vmem((4, FN, FR, LANES)),
            vmem((4, CN, CR, LANES)),
        ]
        + [vmem((2, r, LANES)) for r in (5 * FR, COARSE_ROWS, 8 * FR) for _ in range(2)]
        + [pltpu.SemaphoreType.DMA((n,)) for n in (14, 4, 2, 2, 2, 2, 2, 2)],
        compiler_params=pltpu.CompilerParams(
            collective_id=0, has_side_effects=True, vmem_limit_bytes=63 * 1024 * 1024
        ),
        name="smooth",
    )(spots, cu, cp, cm, cf, fu, fp, fm, ff)
    fvel, fpres, cvel, cpres = pl.pallas_call(
        place_kernel,
        out_shape=tuple(jax.ShapeDtypeStruct(a.shape, F32) for a in (fu, fp, cu, cp)),
        in_specs=[smem_spec, vmem_spec, vmem_spec],
        out_specs=(vmem_spec,) * 4,
        compiler_params=pltpu.CompilerParams(vmem_limit_bytes=63 * 1024 * 1024),
        name="place",
    )(spots, fine, coarse)
    return (
        cvel.transpose(0, 1, 3, 2),
        cpres.transpose(0, 2, 1),
        fvel[:, :, None],
        fpres[:, None],
    )


def solution(mesh):
    groups, subs = mesh.shape["boxgrp"], mesh.shape["sub"]
    zs = ("boxgrp", "sub")
    return jax.shard_map(
        functools.partial(on_device, groups, subs),
        mesh=mesh,
        in_specs=(
            P(None, zs, None, None),
            P(zs, None, None),
            P(zs, None, None),
            P(None, zs, None, None),
            P(None, "sub", "boxgrp", None, None),
            P("sub", "boxgrp", None, None),
            P("sub", "boxgrp", None, None),
            P(None, "sub", "boxgrp", None, None),
            P(),
        ),
        out_specs=(
            P(None, zs, None, None),
            P(zs, None, None),
            P(None, "sub", "boxgrp", None, None),
            P("sub", "boxgrp", None, None),
        ),
        check_vma=False,
    )
```

```python
import functools

import jax
import jax.numpy as jnp
from jax import lax
from jax.experimental import pallas as pl
from jax.experimental.pallas import tpu as pltpu
from jax.sharding import PartitionSpec as P

MESH = pl.DeviceIdType.MESH
F32 = jnp.float32
BF16 = jnp.bfloat16

HALF = 64
LANES = 128
TOP = 8

FN, FR = 8, 32
CN, CR = 4, 16

OFF = 4
DEEP = 4

UZ, UR, UL, PR, MU, TZ, TR, DA, U1, U2 = range(10)
TL, RI, RV, S0, F0, F1, F2, VF = 0, 1, 2, 3, 4, 5, 6, 7
FLAT = VF + 6

COARSE_MSG = (
    (UZ, True, 4),
    (PR, True, 4),
    (MU, True, 4),
    (UR, True, 3),
    (UL, True, 3),
    (F0, False, 3),
    (F1, False, 2),
    (F2, False, 2),
)
COARSE_ROWS = CR * sum(depth for _, _, depth in COARSE_MSG)


def lane_of(rows):
    return lax.broadcasted_iota(jnp.int32, (rows, LANES), 1)


def split3(x):
    hi = x.astype(BF16)
    rest = x - hi.astype(F32)
    mid = rest.astype(BF16)
    low = (rest - mid.astype(F32)).astype(BF16)
    return hi, mid, low


def pick_nt(sel, data):
    dims = (((1,), (1,)), ((), ()))
    return sum(
        lax.dot_general(sel, part, dims, preferred_element_type=F32) for part in split3(data)
    )


def pick_nn(data, sel):
    dims = (((1,), (0,)), ((), ()))
    return sum(
        lax.dot_general(part, sel, dims, preferred_element_type=F32) for part in split3(data)
    )


def one_where(cond):
    return jnp.where(cond, 1.0, 0.0).astype(BF16)


class Level:
    def __init__(self, planes, rows, inv_sq, inv_two, pad, flat):
        self.n, self.rows, self.inv_sq, self.inv_two = planes, rows, inv_sq, inv_two
        self.pad, self.flat = pad, flat
        lane = lane_of(rows) % HALF
        self.first = lane == 0
        self.last = lane == HALF - 1

    def mid(self, slot, z):
        return self.pad[slot, z + OFF, TOP : TOP + self.rows, :]

    def row_dn(self, slot, z):
        return self.pad[slot, z + OFF, TOP - 1 : TOP - 1 + self.rows, :]

    def row_up(self, slot, z):
        return self.pad[slot, z + OFF, TOP + 1 : TOP + 1 + self.rows, :]

    def lane_dn(self, x):
        return jnp.where(self.first, 0.0, pltpu.roll(x, 1, 1))

    def lane_up(self, x):
        return jnp.where(self.last, 0.0, pltpu.roll(x, LANES - 1, 1))

    def get(self, slot, z):
        return self.flat[slot, z + OFF]

    def keep(self, slot, z, x):
        self.flat[slot, z + OFF] = x

    def set_mid(self, slot, z, x):
        self.pad[slot, z + OFF, TOP : TOP + self.rows, :] = x

    def put(self, slot, z, x, ghost_lo=0.0, ghost_hi=0.0):
        self.set_mid(slot, z, x)
        left = lane_of(1) < HALF
        head = pltpu.roll(x[0:1], HALF, 1)
        tail = pltpu.roll(x[self.rows - 1 : self.rows], HALF, 1)
        self.pad[slot, z + OFF, TOP - 1 : TOP, :] = jnp.where(left, ghost_lo, tail)
        self.pad[slot, z + OFF, TOP + self.rows : TOP + self.rows + 1, :] = jnp.where(
            left, head, ghost_hi
        )

    def around(self, slot, z):
        x = self.mid(slot, z)
        return x, [
            self.mid(slot, z - 1),
            self.mid(slot, z + 1),
            self.row_dn(slot, z),
            self.row_up(slot, z),
            self.lane_dn(x),
            self.lane_up(x),
        ]

    def relax(self, z, full=True, drop=None):
        def kept(x):
            return x if drop is None else jnp.where(drop, 0.0, x)

        mu, nb = self.around(MU, z)
        sums = [mu + m for m in nb]
        total = (sums[0] + sums[1]) + (sums[2] + sums[3]) + (sums[4] + sums[5])
        half = 0.5 * self.inv_sq
        diag = (1.25 * half) * total
        inv = 1.0 / diag
        _, pres = self.around(PR, z)
        out = []
        for comp, slot in enumerate((UZ, UR, UL) if full else (UZ,)):
            u, nb = self.around(slot, z)
            prod = [s * v for s, v in zip(sums, nb)]
            acc = (prod[0] + prod[1]) + (prod[2] + prod[3]) + (prod[4] + prod[5])
            grad = self.inv_two * (pres[2 * comp + 1] - pres[2 * comp])
            out.append(0.2 * u + (self.get(F0 + comp, z) - grad + half * acc) * inv)
        self.set_mid(TZ, z, kept(out[0]))
        self.put(DA, z, kept(diag))
        self.keep(RI, z, inv)
        if full:
            end = TOP + self.rows
            self.put(
                TR,
                z,
                out[1],
                self.pad[UR, z + OFF, TOP - 1 : TOP, :],
                self.pad[UR, z + OFF, end : end + 1, :],
            )
            self.keep(TL, z, out[2])
            self.keep(
                S0,
                z,
                (self.row_up(TR, z) - self.row_dn(TR, z))
                + (self.lane_up(out[2]) - self.lane_dn(out[2])),
            )

    def first_update(self, z, drop=None):
        div = (self.mid(TZ, z + 1) - self.mid(TZ, z - 1)) + self.get(S0, z)
        diag, nb = self.around(DA, z)
        faces = [1.0 / (diag + d) for d in nb]
        inv = 1.0 / ((faces[0] + faces[1]) + (faces[2] + faces[3]) + (faces[4] + faces[5]))
        for i, face in enumerate(faces):
            self.keep(VF + i, z, face)
        self.keep(RV, z, inv)
        value = (-0.4 * self.inv_two / self.inv_sq) * div * inv
        self.put(U1, z, value if drop is None else jnp.where(drop, 0.0, value))

    def sweep(self, z, drop=None):
        u, nb = self.around(U1, z)
        prod = [self.get(VF + i, z) * v for i, v in enumerate(nb)]
        acc = (prod[0] + prod[1]) + (prod[2] + prod[3]) + (prod[4] + prod[5])
        value = 1.2 * u + (0.8 * self.get(RV, z)) * acc
        self.put(U2, z, value if drop is None else jnp.where(drop, 0.0, value))

    def finish(self, z):
        u, nb = self.around(U2, z)
        inv = self.inv_two * self.get(RI, z)
        tees = (self.mid(TZ, z), self.mid(TR, z), self.get(TL, z))
        vel = [t - (nb[2 * i + 1] - nb[2 * i]) * inv for i, t in enumerate(tees)]
        return vel, self.mid(PR, z) + u


def packed(raw, rows):
    return jnp.concatenate([raw[0:rows], raw[rows : 2 * rows]], axis=1)


def smooth_kernel(
    groups,
    subs,
    spots,
    cu_hbm,
    cp_hbm,
    cm_hbm,
    cf_hbm,
    fu_hbm,
    fp_hbm,
    fm_hbm,
    ff_hbm,
    fine_out,
    coarse_out,
    spot_out,
    cu,
    cp,
    cm,
    cf,
    fu,
    fp,
    fm,
    ff,
    fpad,
    fflat,
    cpad,
    cflat,
    sb1,
    rb1,
    sbc,
    rbc,
    sb2,
    rb2,
    in_sem,
    send1,
    recv1,
    sendc,
    recvc,
    send2,
    recv2,
):
    g = lax.axis_index("boxgrp")
    s = lax.axis_index("sub")
    up_g, up_s = lax.rem(g + (s + 1) // subs, groups), lax.rem(s + 1, subs)
    down_g = lax.rem(g + (groups - 1) + (s + subs - 1) // subs, groups)
    down_s = lax.rem(s + subs - 1, subs)
    dev = g * subs + s
    has_up = dev < groups * subs - 1
    has_down = dev > 0
    box_low = s == 0
    box_high = s == subs - 1

    barrier = pltpu.get_barrier_semaphore()

    @pl.when(has_up)
    def _():
        pl.semaphore_signal(barrier, inc=1, device_id=(up_g, up_s), device_id_type=MESH)

    @pl.when(has_down)
    def _():
        pl.semaphore_signal(barrier, inc=1, device_id=(down_g, down_s), device_id_type=MESH)

    loads = []

    def load(src, dst):
        copy = pltpu.make_async_copy(src, dst, in_sem.at[len(loads)])
        copy.start()
        loads.append(copy)

    for z in (0, FN - 1):
        load(fu_hbm.at[:, z], fu.at[:, z])
        load(fp_hbm.at[z], fp.at[z])
        load(fm_hbm.at[z], fm.at[z])
    for src, dst in ((cu_hbm, cu), (cp_hbm, cp), (cm_hbm, cm), (cf_hbm, cf)):
        load(src, dst)
    inner = pl.ds(1, FN - 2)
    load(fu_hbm.at[:, inner], fu.at[:, inner])
    load(fp_hbm.at[inner], fp.at[inner])
    load(fm_hbm.at[inner], fm.at[inner])
    load(ff_hbm, ff)

    fine = Level(FN, FR, 4.0, 1.0, fpad, fflat)
    coarse = Level(CN, CR, 1.0, 0.5, cpad, cflat)

    def fine_raw(slot, z):
        if slot < PR:
            return fu[slot, z]
        return fp[z] if slot == PR else fm[z]

    def coarse_raw(slot, k):
        if slot in (UZ, UR, UL):
            return cu[(0, 2, 1)[slot], k]
        return cp[k] if slot == PR else cm[k]

    def for_fine(slot, k):
        if slot < PR:
            return cu[slot, k]
        return cp[k] if slot == PR else cm[k]

    def remote(sb, rb, send, recv, side):
        return pltpu.make_async_remote_copy(
            src_ref=sb.at[side],
            dst_ref=rb.at[side],
            send_sem=send.at[side],
            recv_sem=recv.at[side],
            device_id=(
                jnp.where(side == 0, up_g, down_g),
                jnp.where(side == 0, up_s, down_s),
            ),
            device_id_type=MESH,
        )

    for copy in loads[0:6]:
        copy.wait()
    for slot in range(5):
        at = slice(slot * FR, (slot + 1) * FR)
        sb1[0, at, :] = packed(fine_raw(slot, FN - 1), FR)
        sb1[1, at, :] = packed(fine_raw(slot, 0), FR)

    @pl.when(has_up & has_down)
    def _():
        pl.semaphore_wait(barrier, 2)

    @pl.when(~(has_up & has_down))
    def _():
        pl.semaphore_wait(barrier, 1)

    one_up = remote(sb1, rb1, send1, recv1, 0)
    one_down = remote(sb1, rb1, send1, recv1, 1)
    pl.when(s < subs - 1)(one_up.start)
    pl.when(s > 0)(one_down.start)

    for copy in loads[6:10]:
        copy.wait()

    @pl.when(box_low | box_high)
    def _():
        q_edge = jnp.where(
            box_high, spots[lax.rem(g + 1, groups)], spots[lax.rem(g + groups - 1, groups)]
        )
        q_edge = jnp.maximum(q_edge, 0)
        row = lax.broadcasted_iota(jnp.int32, (2 * FR, HALF), 0)
        col = lax.broadcasted_iota(jnp.int32, (2 * FR, HALF), 1)
        pick_y = one_where(col == 32 * q_edge + row // 2)
        row = lax.broadcasted_iota(jnp.int32, (32, LANES), 0)
        col = lax.broadcasted_iota(jnp.int32, (32, LANES), 1)
        pick_x = one_where(row == (col % HALF) // 2)
        ghost = []
        for slot in range(5):
            plane = jnp.where(box_high, for_fine(slot, CN - 1), for_fine(slot, 0))
            ghost.append(pick_nt(pick_y, plane))
        ghost = pick_nn(jnp.concatenate(ghost, axis=0), pick_x)
        left = lane_of(FR) < HALF
        side = jnp.where(box_high, 0, 1)
        for i in range(5):
            sb1[side, i * FR : (i + 1) * FR, :] = jnp.where(
                left, ghost[64 * i : 64 * i + 32], ghost[64 * i + 32 : 64 * i + 64]
            )

    pl.when(box_high & has_up)(one_up.start)
    pl.when(box_low & has_down)(one_down.start)

    for k in range(CN):
        for slot in range(5):
            coarse.put(slot, k, packed(coarse_raw(slot, k), CR))
        for comp in range(3):
            coarse.keep(F0 + comp, k, packed(cf[(0, 2, 1)[comp], k], CR))
    base = 0
    for slot, padded, depth in COARSE_MSG:
        read = coarse.mid if padded else coarse.get
        for d in range(depth):
            sbc[0, base : base + CR, :] = read(slot, CN - 1 - d)
            sbc[1, base : base + CR, :] = read(slot, d)
            base += CR
    deep_up = remote(sbc, rbc, sendc, recvc, 0)
    deep_down = remote(sbc, rbc, sendc, recvc, 1)
    pl.when(has_up)(deep_up.start)
    pl.when(has_down)(deep_down.start)

    q_own = spots[g]
    filled = q_own >= 0
    spot_out[...] = jnp.full((8, LANES), q_own, jnp.int32)
    col = lax.broadcasted_iota(jnp.int32, (16, HALF), 1)
    pick_row = one_where(col == jnp.where(q_own == 1, 31, 32))
    rows = []
    for slot in range(5):
        planes = jnp.concatenate([for_fine(slot, k) for k in range(CN)], axis=0)
        rows.append(pick_nt(pick_row, planes))
    row = lax.broadcasted_iota(jnp.int32, (LANES, CN * LANES), 0)
    col = lax.broadcasted_iota(jnp.int32, (LANES, CN * LANES), 1)
    pick_k = one_where(row == 32 * (col // LANES) + (col % HALF) // 2)
    rows = pick_nn(jnp.concatenate(rows, axis=0), pick_k)

    for copy in loads[10:14]:
        copy.wait()
    for z in range(FN):
        for slot in range(5):
            k = z // 2
            line = rows[16 * slot : 16 * slot + 1, LANES * k : LANES * (k + 1)]
            lo = jnp.where(q_own == 1, line, 0.0)
            hi = jnp.where(q_own == 1, 0.0, line)
            fine.put(slot, z, packed(fine_raw(slot, z), FR), lo, hi)
        for comp in range(3):
            fine.keep(F0 + comp, z, packed(ff[comp, z], FR))

    for z in range(1, FN - 1):
        fine.relax(z)

    for step in range(2):
        side = jnp.where(s < subs // 2, 1 - step, step)
        low = side == 0
        there = (low & has_down) | ((side == 1) & has_up)
        pl.when(there)(remote(sb1, rb1, send1, recv1, side).wait_recv)
        edge = jnp.where(low, 0, FN - 1)
        beyond = jnp.where(low, -1, FN)
        for slot in range(5):
            value = rb1[side, slot * FR : (slot + 1) * FR, :]
            fine.set_mid(slot, beyond, jnp.where(there, value, 0.0))
        fine.relax(edge)
        inward = jnp.where(low, 1, -1)
        back = 1 - side
        for d in range(3):
            sb2[back, d * FR : (d + 1) * FR, :] = fine.mid(TZ, edge + inward * d)
            sb2[back, (3 + d) * FR : (4 + d) * FR, :] = fine.mid(DA, edge + inward * d)
        for d in range(2):
            sb2[back, (6 + d) * FR : (7 + d) * FR, :] = fine.get(S0, edge + inward * d)
        same_box = (low & (s > 0)) | ((side == 1) & (s < subs - 1))
        pl.when(same_box)(remote(sb2, rb2, send2, recv2, back).start)

    def fine_finish(z):
        vel, pres = fine.finish(z)
        for i in range(3):
            fine_out[i, z] = jnp.where(filled, vel[i], 0.0)
        fine_out[3, z] = jnp.where(filled, pres, 0.0)

    for z in range(1, FN - 1):
        fine.first_update(z)
    for z in range(2, FN - 2):
        fine.sweep(z)
    for z in range(3, FN - 3):
        fine_finish(z)

    pl.when(has_down)(deep_up.wait_recv)
    pl.when(has_up)(deep_down.wait_recv)
    base = 0
    for slot, padded, depth in COARSE_MSG:
        write = coarse.put if padded else coarse.keep
        for d in range(depth):
            at = slice(base, base + CR)
            write(slot, -1 - d, jnp.where(has_down, rbc[0, at, :], 0.0))
            write(slot, CN + d, jnp.where(has_up, rbc[1, at, :], 0.0))
            base += CR
    no_down, no_up = dev == 0, dev == groups * subs - 1
    coarse.relax(-3, False, no_down)
    coarse.relax(CN + 2, False, no_up)
    for d in (2, 1):
        coarse.relax(-d, True, no_down)
        coarse.relax(CN - 1 + d, True, no_up)
    for z in range(CN):
        coarse.relax(z)
    for d in (2, 1):
        coarse.first_update(-d, no_down)
        coarse.first_update(CN - 1 + d, no_up)
    for z in range(CN):
        coarse.first_update(z)
    coarse.sweep(-1, no_down)
    coarse.sweep(CN, no_up)
    for z in range(CN):
        coarse.sweep(z)
    for z in range(CN):
        vel, pres = coarse.finish(z)
        for i, c in enumerate((0, 2, 1)):
            coarse_out[c, z] = vel[i]
        coarse_out[3, z] = pres

    pl.when(s > 0)(remote(sb2, rb2, send2, recv2, 0).wait_recv)
    pl.when(s < subs - 1)(remote(sb2, rb2, send2, recv2, 1).wait_recv)
    for side, end, beyond, way in ((0, box_low, -1, -1), (1, box_high, FN, 1)):
        for d in range(3):
            z = beyond + way * d
            tz = rb2[side, d * FR : (d + 1) * FR, :]
            fine.set_mid(TZ, z, jnp.where(end, fine.mid(UZ, beyond), tz))
            diag = rb2[side, (3 + d) * FR : (4 + d) * FR, :]
            fine.put(DA, z, jnp.where(end, 0.0, diag))
            if d < 2:
                fine.keep(S0, z, rb2[side, (6 + d) * FR : (7 + d) * FR, :])
    fine.first_update(0)
    fine.first_update(FN - 1)
    for d in (1, 2):
        fine.first_update(-d, box_low)
        fine.first_update(FN - 1 + d, box_high)
    fine.sweep(-1, box_low)
    fine.sweep(FN, box_high)
    for z in (0, 1, FN - 2, FN - 1):
        fine.sweep(z)
    for z in (0, 1, 2):
        fine_finish(z)
    for z in (FN - 3, FN - 2, FN - 1):
        fine_finish(z)

    pl.when(has_up)(one_up.wait_send)
    pl.when(has_down)(one_down.wait_send)
    pl.when(has_up)(deep_up.wait_send)
    pl.when(has_down)(deep_down.wait_send)
    pl.when(s < subs - 1)(remote(sb2, rb2, send2, recv2, 0).wait_send)
    pl.when(s > 0)(remote(sb2, rb2, send2, recv2, 1).wait_send)


def place_kernel(
    fine_in, coarse_in, spot_in, fvel_hbm, fpres_hbm, cvel_hbm, cpres_hbm, fbuf, cbuf, sem
):
    copies = []

    def send(src, dst):
        copy = pltpu.make_async_copy(src, dst, sem.at[len(copies)])
        copy.start()
        copies.append(copy)

    for f in range(4):
        for z in range(FN):
            x = fine_in[f, z]
            fbuf[f, z, 0:FR, :] = x[:, 0:HALF]
            fbuf[f, z, FR : 2 * FR, :] = x[:, HALF:LANES]
        send(fbuf.at[f], fvel_hbm.at[f] if f < 3 else fpres_hbm)
    row = lax.broadcasted_iota(jnp.int32, (32, HALF), 0)
    col = lax.broadcasted_iota(jnp.int32, (32, HALF), 1)
    mean = jnp.where(row == col // 2, 0.125, 0.0).astype(BF16)
    lane = lane_of(32)
    covers = col // 32 == spot_in[0:1, 0:HALF]
    for f in range(4):
        pairs = []
        for k in range(CN):
            parts = [
                fbuf[f, z, pl.ds(start, FR, stride=2), :]
                for z in (2 * k, 2 * k + 1)
                for start in range(2)
            ]
            pairs.append((parts[0] + parts[1]) + (parts[2] + parts[3]))
        blk = pick_nt(mean, jnp.concatenate(pairs, axis=0))
        for k in range(CN):
            lo = pltpu.roll(blk, (LANES - 32 * k) % LANES, 1) if k else blk
            hi = pltpu.roll(blk, (LANES + 32 - 32 * k) % LANES, 1) if k != 1 else blk
            x = coarse_in[f, k]
            own = jnp.concatenate([x[:, 0:HALF], x[:, HALF:LANES]], axis=0)
            cbuf[f, k] = jnp.where(covers, jnp.where(lane < 32, lo, hi)[:, 0:HALF], own)
    send(cbuf.at[pl.ds(0, 3)], cvel_hbm)
    send(cbuf.at[3], cpres_hbm)
    for copy in copies:
        copy.wait()


def on_device(groups, subs, cu, cp, cm, cf, fu, fp, fm, ff, spots):
    cu, cf = [a.transpose(0, 1, 3, 2) for a in (cu, cf)]
    cp, cm = [a.transpose(0, 2, 1) for a in (cp, cm)]
    fu, ff = [a[:, :, 0] for a in (fu, ff)]
    fp, fm = [a[:, 0] for a in (fp, fm)]
    vmem = functools.partial(pltpu.VMEM, dtype=F32)
    smem_spec = pl.BlockSpec(memory_space=pltpu.SMEM)
    hbm_spec = pl.BlockSpec(memory_space=pltpu.HBM)
    vmem_spec = pl.BlockSpec(memory_space=pltpu.VMEM)
    fine, coarse, spot = pl.pallas_call(
        functools.partial(smooth_kernel, groups, subs),
        out_shape=(
            pltpu.VMEM((4, FN, FR, LANES), F32),
            pltpu.VMEM((4, CN, CR, LANES), F32),
            pltpu.VMEM((8, LANES), jnp.int32),
        ),
        in_specs=[smem_spec] + [hbm_spec] * 8,
        out_specs=(vmem_spec,) * 3,
        scratch_shapes=[vmem(a.shape) for a in (cu, cp, cm, cf, fu, fp, fm, ff)]
        + [
            vmem((10, FN + 2 * OFF, FR + 16, LANES)),
            vmem((FLAT, FN + 2 * OFF, FR, LANES)),
            vmem((10, CN + 2 * OFF, CR + 16, LANES)),
            vmem((FLAT, CN + 2 * OFF, CR, LANES)),
        ]
        + [vmem((2, r, LANES)) for r in (5 * FR, COARSE_ROWS, 8 * FR) for _ in range(2)]
        + [pltpu.SemaphoreType.DMA((n,)) for n in (14, 2, 2, 2, 2, 2, 2)],
        compiler_params=pltpu.CompilerParams(
            collective_id=0, has_side_effects=True, vmem_limit_bytes=62 * 1024 * 1024
        ),
        name="smooth",
    )(spots, cu, cp, cm, cf, fu, fp, fm, ff)
    fvel, fpres, cvel, cpres = pl.pallas_call(
        place_kernel,
        out_shape=tuple(jax.ShapeDtypeStruct(a.shape, F32) for a in (fu, fp, cu, cp)),
        in_specs=[vmem_spec] * 3,
        out_specs=(hbm_spec,) * 4,
        scratch_shapes=[
            vmem((4, FN, 2 * FR, HALF)),
            vmem((4, CN, 2 * CR, HALF)),
            pltpu.SemaphoreType.DMA((6,)),
        ],
        compiler_params=pltpu.CompilerParams(vmem_limit_bytes=16 * 1024 * 1024),
        name="place",
    )(fine, coarse, spot)
    return (
        cvel.transpose(0, 1, 3, 2),
        cpres.transpose(0, 2, 1),
        fvel[:, :, None],
        fpres[:, None],
    )


def solution(mesh):
    groups, subs = mesh.shape["boxgrp"], mesh.shape["sub"]
    zs = ("boxgrp", "sub")
    return jax.shard_map(
        functools.partial(on_device, groups, subs),
        mesh=mesh,
        in_specs=(
            P(None, zs, None, None),
            P(zs, None, None),
            P(zs, None, None),
            P(None, zs, None, None),
            P(None, "sub", "boxgrp", None, None),
            P("sub", "boxgrp", None, None),
            P("sub", "boxgrp", None, None),
            P(None, "sub", "boxgrp", None, None),
            P(),
        ),
        out_specs=(
            P(None, zs, None, None),
            P(zs, None, None),
            P(None, "sub", "boxgrp", None, None),
            P("sub", "boxgrp", None, None),
        ),
        check_vma=False,
    )
```

```python
import functools

import jax
import jax.numpy as jnp
from jax import lax
from jax.experimental import pallas as pl
from jax.experimental.pallas import tpu as pltpu
from jax.sharding import PartitionSpec as P

MESH = pl.DeviceIdType.MESH
F32 = jnp.float32
BF16 = jnp.bfloat16

HALF = 64
LANES = 128
TOP = 8

FN, FR = 8, 32
CN, CR = 4, 16

OFF = 4
DEEP = 4

UZ, UR, UL, PR, MU, TZ, TR, DA, U1, U2 = range(10)
TL, RI, RV, S0, F0, F1, F2, VF = 0, 1, 2, 3, 4, 5, 6, 7
FLAT = VF + 6

COARSE_MSG = (
    (UZ, True, 4),
    (PR, True, 4),
    (MU, True, 4),
    (UR, True, 3),
    (UL, True, 3),
    (F0, False, 3),
    (F1, False, 2),
    (F2, False, 2),
)
COARSE_ROWS = CR * sum(depth for _, _, depth in COARSE_MSG)


def lane_of(rows):
    return lax.broadcasted_iota(jnp.int32, (rows, LANES), 1)


def split3(x):
    hi = x.astype(BF16)
    rest = x - hi.astype(F32)
    mid = rest.astype(BF16)
    low = (rest - mid.astype(F32)).astype(BF16)
    return hi, mid, low


def pick_nt(sel, data):
    dims = (((1,), (1,)), ((), ()))
    return sum(
        lax.dot_general(sel, part, dims, preferred_element_type=F32) for part in split3(data)
    )


def pick_nn(data, sel):
    dims = (((1,), (0,)), ((), ()))
    return sum(
        lax.dot_general(part, sel, dims, preferred_element_type=F32) for part in split3(data)
    )


def one_where(cond):
    return jnp.where(cond, 1.0, 0.0).astype(BF16)


class Level:
    def __init__(self, planes, rows, inv_sq, inv_two, pad, flat):
        self.n, self.rows, self.inv_sq, self.inv_two = planes, rows, inv_sq, inv_two
        self.pad, self.flat = pad, flat
        lane = lane_of(rows) % HALF
        self.first = lane == 0
        self.last = lane == HALF - 1

    def span(self, z, shift):
        start = (z + OFF) * (self.rows + 2 * TOP) + TOP + shift
        return slice(start, start + self.rows)

    def mid(self, slot, z):
        return self.pad[slot][self.span(z, 0), :]

    def row_dn(self, slot, z):
        return self.pad[slot][self.span(z, -1), :]

    def row_up(self, slot, z):
        return self.pad[slot][self.span(z, 1), :]

    def lane_dn(self, x):
        return jnp.where(self.first, 0.0, pltpu.roll(x, 1, 1))

    def lane_up(self, x):
        return jnp.where(self.last, 0.0, pltpu.roll(x, LANES - 1, 1))

    def get(self, slot, z):
        return self.flat[slot][z + OFF]

    def keep(self, slot, z, x):
        self.flat[slot][z + OFF] = x

    def set_mid(self, slot, z, x):
        self.pad[slot][self.span(z, 0), :] = x

    def seam_rows(self, slot, z0):
        pitch = self.rows + 2 * TOP
        ref = self.pad[slot]
        base = (z0 + OFF) * pitch
        ends = (TOP - 1, TOP, TOP + self.rows - 1, TOP + self.rows)
        return ref, [pl.ds(base + row, 8, stride=pitch) for row in ends]

    def seam(self, slot, z0, ghost_lo=0.0, ghost_hi=0.0):
        ref, (below, first, last, above) = self.seam_rows(slot, z0)
        left = lane_of(8) < HALF
        tail = pltpu.roll(ref[last, :], HALF, 1)
        head = pltpu.roll(ref[first, :], HALF, 1)
        ref[below, :] = jnp.where(left, ghost_lo, tail)
        ref[above, :] = jnp.where(left, head, ghost_hi)

    def seam_relaxed(self, z0):
        ref, (below, _, _, above) = self.seam_rows(UR, z0)
        self.seam(TR, z0, ref[below, :], ref[above, :])
        self.seam(DA, z0)

    def around(self, slot, z):
        x = self.mid(slot, z)
        return x, [
            self.mid(slot, z - 1),
            self.mid(slot, z + 1),
            self.row_dn(slot, z),
            self.row_up(slot, z),
            self.lane_dn(x),
            self.lane_up(x),
        ]

    def relax(self, z, full=True, drop=None):
        def kept(x):
            return x if drop is None else jnp.where(drop, 0.0, x)

        mu, nb = self.around(MU, z)
        sums = [mu + m for m in nb]
        total = (sums[0] + sums[1]) + (sums[2] + sums[3]) + (sums[4] + sums[5])
        half = 0.5 * self.inv_sq
        diag = (1.25 * half) * total
        inv = 1.0 / diag
        _, pres = self.around(PR, z)
        out = []
        for comp, slot in enumerate((UZ, UR, UL) if full else (UZ,)):
            u, nb = self.around(slot, z)
            prod = [s * v for s, v in zip(sums, nb)]
            acc = (prod[0] + prod[1]) + (prod[2] + prod[3]) + (prod[4] + prod[5])
            grad = self.inv_two * (pres[2 * comp + 1] - pres[2 * comp])
            out.append(0.2 * u + (self.get(F0 + comp, z) - grad + half * acc) * inv)
        self.set_mid(TZ, z, kept(out[0]))
        self.set_mid(DA, z, kept(diag))
        self.keep(RI, z, inv)
        if full:
            self.set_mid(TR, z, out[1])
            self.keep(TL, z, out[2])

    def in_plane(self, z):
        tl = self.get(TL, z)
        rows = self.row_up(TR, z) - self.row_dn(TR, z)
        self.keep(S0, z, rows + (self.lane_up(tl) - self.lane_dn(tl)))

    def first_update(self, z, drop=None):
        div = (self.mid(TZ, z + 1) - self.mid(TZ, z - 1)) + self.get(S0, z)
        diag, nb = self.around(DA, z)
        faces = [1.0 / (diag + d) for d in nb]
        inv = 1.0 / ((faces[0] + faces[1]) + (faces[2] + faces[3]) + (faces[4] + faces[5]))
        for i, face in enumerate(faces):
            self.keep(VF + i, z, face)
        self.keep(RV, z, inv)
        value = (-0.4 * self.inv_two / self.inv_sq) * div * inv
        self.set_mid(U1, z, value if drop is None else jnp.where(drop, 0.0, value))

    def sweep(self, z, drop=None):
        u, nb = self.around(U1, z)
        prod = [self.get(VF + i, z) * v for i, v in enumerate(nb)]
        acc = (prod[0] + prod[1]) + (prod[2] + prod[3]) + (prod[4] + prod[5])
        value = 1.2 * u + (0.8 * self.get(RV, z)) * acc
        self.set_mid(U2, z, value if drop is None else jnp.where(drop, 0.0, value))

    def finish(self, z):
        u, nb = self.around(U2, z)
        inv = self.inv_two * self.get(RI, z)
        tees = (self.mid(TZ, z), self.mid(TR, z), self.get(TL, z))
        vel = [t - (nb[2 * i + 1] - nb[2 * i]) * inv for i, t in enumerate(tees)]
        return vel, self.mid(PR, z) + u


def packed(raw, rows):
    return jnp.concatenate([raw[0:rows], raw[rows : 2 * rows]], axis=1)


def smooth_kernel(
    groups,
    subs,
    spots,
    cu_hbm,
    cp_hbm,
    cm_hbm,
    cf_hbm,
    fu_hbm,
    fp_hbm,
    fm_hbm,
    ff_hbm,
    fine_out,
    coarse_out,
    spot_out,
    cu,
    cp,
    cm,
    cf,
    fu,
    fp,
    fm,
    ff,
    fpad,
    fflat,
    cpad,
    cflat,
    sb1,
    rb1,
    sbc,
    rbc,
    sb2,
    rb2,
    in_sem,
    send1,
    recv1,
    sendc,
    recvc,
    send2,
    recv2,
):
    g = lax.axis_index("boxgrp")
    s = lax.axis_index("sub")
    up_g, up_s = lax.rem(g + (s + 1) // subs, groups), lax.rem(s + 1, subs)
    down_g = lax.rem(g + (groups - 1) + (s + subs - 1) // subs, groups)
    down_s = lax.rem(s + subs - 1, subs)
    dev = g * subs + s
    has_up = dev < groups * subs - 1
    has_down = dev > 0
    box_low = s == 0
    box_high = s == subs - 1

    barrier = pltpu.get_barrier_semaphore()

    @pl.when(has_up)
    def _():
        pl.semaphore_signal(barrier, inc=1, device_id=(up_g, up_s), device_id_type=MESH)

    @pl.when(has_down)
    def _():
        pl.semaphore_signal(barrier, inc=1, device_id=(down_g, down_s), device_id_type=MESH)

    loads = []

    def load(src, dst):
        copy = pltpu.make_async_copy(src, dst, in_sem.at[len(loads)])
        copy.start()
        loads.append(copy)

    for z in (0, FN - 1):
        load(fu_hbm.at[:, z], fu.at[:, z])
        load(fp_hbm.at[z], fp.at[z])
        load(fm_hbm.at[z], fm.at[z])
    for src, dst in ((cu_hbm, cu), (cp_hbm, cp), (cm_hbm, cm), (cf_hbm, cf)):
        load(src, dst)
    inner = pl.ds(1, FN - 2)
    load(fu_hbm.at[:, inner], fu.at[:, inner])
    load(fp_hbm.at[inner], fp.at[inner])
    load(fm_hbm.at[inner], fm.at[inner])
    load(ff_hbm, ff)

    fine = Level(FN, FR, 4.0, 1.0, fpad, fflat)
    coarse = Level(CN, CR, 1.0, 0.5, cpad, cflat)

    def fine_raw(slot, z):
        if slot < PR:
            return fu[slot, z]
        return fp[z] if slot == PR else fm[z]

    def coarse_raw(slot, k):
        if slot in (UZ, UR, UL):
            return cu[(0, 2, 1)[slot], k]
        return cp[k] if slot == PR else cm[k]

    def for_fine(slot, k):
        if slot < PR:
            return cu[slot, k]
        return cp[k] if slot == PR else cm[k]

    def remote(sb, rb, send, recv, side):
        return pltpu.make_async_remote_copy(
            src_ref=sb.at[side],
            dst_ref=rb.at[side],
            send_sem=send.at[side],
            recv_sem=recv.at[side],
            device_id=(down_g, down_s) if side else (up_g, up_s),
            device_id_type=MESH,
        )

    for copy in loads[0:6]:
        copy.wait()
    for slot in range(5):
        at = slice(slot * FR, (slot + 1) * FR)
        sb1[0, at, :] = packed(fine_raw(slot, FN - 1), FR)
        sb1[1, at, :] = packed(fine_raw(slot, 0), FR)

    @pl.when(has_up & has_down)
    def _():
        pl.semaphore_wait(barrier, 2)

    @pl.when(~(has_up & has_down))
    def _():
        pl.semaphore_wait(barrier, 1)

    one_up = remote(sb1, rb1, send1, recv1, 0)
    one_down = remote(sb1, rb1, send1, recv1, 1)
    pl.when(s < subs - 1)(one_up.start)
    pl.when(s > 0)(one_down.start)

    for copy in loads[6:10]:
        copy.wait()

    @pl.when(box_low | box_high)
    def _():
        q_edge = jnp.where(
            box_high, spots[lax.rem(g + 1, groups)], spots[lax.rem(g + groups - 1, groups)]
        )
        q_edge = jnp.maximum(q_edge, 0)
        row = lax.broadcasted_iota(jnp.int32, (2 * FR, HALF), 0)
        col = lax.broadcasted_iota(jnp.int32, (2 * FR, HALF), 1)
        pick_y = one_where(col == 32 * q_edge + row // 2)
        row = lax.broadcasted_iota(jnp.int32, (32, LANES), 0)
        col = lax.broadcasted_iota(jnp.int32, (32, LANES), 1)
        pick_x = one_where(row == (col % HALF) // 2)
        ghost = []
        for slot in range(5):
            plane = jnp.where(box_high, for_fine(slot, CN - 1), for_fine(slot, 0))
            ghost.append(pick_nt(pick_y, plane))
        ghost = pick_nn(jnp.concatenate(ghost, axis=0), pick_x)
        left = lane_of(FR) < HALF
        side = jnp.where(box_high, 0, 1)
        for i in range(5):
            sb1[side, i * FR : (i + 1) * FR, :] = jnp.where(
                left, ghost[64 * i : 64 * i + 32], ghost[64 * i + 32 : 64 * i + 64]
            )

    pl.when(box_high & has_up)(one_up.start)
    pl.when(box_low & has_down)(one_down.start)

    for k in range(CN):
        for slot in range(5):
            coarse.set_mid(slot, k, packed(coarse_raw(slot, k), CR))
        for comp in range(3):
            coarse.keep(F0 + comp, k, packed(cf[(0, 2, 1)[comp], k], CR))
    base = 0
    for slot, padded, depth in COARSE_MSG:
        read = coarse.mid if padded else coarse.get
        for d in range(depth):
            sbc[0, base : base + CR, :] = read(slot, CN - 1 - d)
            sbc[1, base : base + CR, :] = read(slot, d)
            base += CR
    deep_up = remote(sbc, rbc, sendc, recvc, 0)
    deep_down = remote(sbc, rbc, sendc, recvc, 1)
    pl.when(has_up)(deep_up.start)
    pl.when(has_down)(deep_down.start)

    q_own = spots[g]
    filled = q_own >= 0
    spot_out[...] = jnp.full((8, LANES), q_own, jnp.int32)
    col = lax.broadcasted_iota(jnp.int32, (16, HALF), 1)
    pick_row = one_where(col == jnp.where(q_own == 1, 31, 32))
    rows = []
    for slot in range(5):
        planes = jnp.concatenate([for_fine(slot, k) for k in range(CN)], axis=0)
        rows.append(pick_nt(pick_row, planes))
    row = lax.broadcasted_iota(jnp.int32, (LANES, CN * LANES), 0)
    col = lax.broadcasted_iota(jnp.int32, (LANES, CN * LANES), 1)
    pick_k = one_where(row == 32 * (col // LANES) + (col % HALF) // 2)
    rows = pick_nn(jnp.concatenate(rows, axis=0), pick_k)

    for copy in loads[10:14]:
        copy.wait()
    for z in range(FN):
        for slot in range(5):
            fine.set_mid(slot, z, packed(fine_raw(slot, z), FR))
        for comp in range(3):
            fine.keep(F0 + comp, z, packed(ff[comp, z], FR))

    above = lax.broadcasted_iota(jnp.int32, (FN, LANES), 0) // 2
    for slot in range(5):
        lines = [rows[16 * slot : 16 * slot + 8, LANES * k : LANES * (k + 1)] for k in range(CN)]
        line = lines[0]
        for k in range(1, CN):
            line = jnp.where(above == k, lines[k], line)
        lo = jnp.where(q_own == 1, line, 0.0)
        hi = jnp.where(q_own == 1, 0.0, line)
        fine.seam(slot, 0, lo, hi)
    for z in range(1, FN - 1):
        fine.relax(z)
    fine.seam_relaxed(0)
    for z in range(1, FN - 1):
        fine.in_plane(z)

    def edge_step(side):
        low = side == 0
        pl.when(has_down if low else has_up)((one_up if low else one_down).wait_recv)
        edge, beyond, inward = (0, -1, 1) if low else (FN - 1, FN, -1)
        for slot in range(5):
            value = rb1[side, slot * FR : (slot + 1) * FR, :]
            value = jnp.where(has_down if low else has_up, value, 0.0)
            fine.set_mid(slot, beyond, value)
        fine.relax(edge)
        fine.seam_relaxed(0)
        fine.in_plane(edge)
        back = 1 - side
        for d in range(3):
            z = edge + inward * d
            sb2[back, d * FR : (d + 1) * FR, :] = fine.mid(TZ, z)
            sb2[back, (3 + d) * FR : (4 + d) * FR, :] = fine.mid(DA, z)
            if d < 2:
                sb2[back, (6 + d) * FR : (7 + d) * FR, :] = fine.get(S0, z)
        pl.when(s > 0 if low else s < subs - 1)((two_down if low else two_up).start)

    two_up = remote(sb2, rb2, send2, recv2, 0)
    two_down = remote(sb2, rb2, send2, recv2, 1)

    @pl.when(s < subs // 2)
    def _():
        edge_step(1)
        edge_step(0)

    @pl.when(s >= subs // 2)
    def _():
        edge_step(0)
        edge_step(1)

    def fine_finish(z):
        vel, pres = fine.finish(z)
        for i in range(3):
            fine_out[i, z] = jnp.where(filled, vel[i], 0.0)
        fine_out[3, z] = jnp.where(filled, pres, 0.0)

    for z in range(1, FN - 1):
        fine.first_update(z)
    fine.seam(U1, 0)
    for z in range(2, FN - 2):
        fine.sweep(z)
    fine.seam(U2, 0)
    for z in range(3, FN - 3):
        fine_finish(z)

    pl.when(has_down)(deep_up.wait_recv)
    pl.when(has_up)(deep_down.wait_recv)
    base = 0
    for slot, padded, depth in COARSE_MSG:
        write = coarse.set_mid if padded else coarse.keep
        for d in range(depth):
            at = slice(base, base + CR)
            write(slot, -1 - d, jnp.where(has_down, rbc[0, at, :], 0.0))
            write(slot, CN + d, jnp.where(has_up, rbc[1, at, :], 0.0))
            base += CR
    for slot in range(5):
        coarse.seam(slot, -OFF)
        coarse.seam(slot, 0)
    no_down, no_up = dev == 0, dev == groups * subs - 1
    coarse.relax(-3, False, no_down)
    coarse.relax(CN + 2, False, no_up)
    for d in (2, 1):
        coarse.relax(-d, True, no_down)
        coarse.relax(CN - 1 + d, True, no_up)
    for z in range(CN):
        coarse.relax(z)
    coarse.seam_relaxed(-OFF)
    coarse.seam_relaxed(0)
    for z in range(-2, CN + 2):
        coarse.in_plane(z)
    for d in (2, 1):
        coarse.first_update(-d, no_down)
        coarse.first_update(CN - 1 + d, no_up)
    for z in range(CN):
        coarse.first_update(z)
    coarse.seam(U1, -2)
    coarse.sweep(-1, no_down)
    coarse.sweep(CN, no_up)
    for z in range(CN):
        coarse.sweep(z)
    coarse.seam(U2, -1)
    for z in range(CN):
        vel, pres = coarse.finish(z)
        for i, c in enumerate((0, 2, 1)):
            coarse_out[c, z] = vel[i]
        coarse_out[3, z] = pres

    pl.when(s > 0)(two_up.wait_recv)
    pl.when(s < subs - 1)(two_down.wait_recv)
    for side, end, beyond, way in ((0, box_low, -1, -1), (1, box_high, FN, 1)):
        for d in range(3):
            z = beyond + way * d
            tz = rb2[side, d * FR : (d + 1) * FR, :]
            fine.set_mid(TZ, z, jnp.where(end, fine.mid(UZ, beyond), tz))
            diag = rb2[side, (3 + d) * FR : (4 + d) * FR, :]
            fine.set_mid(DA, z, jnp.where(end, 0.0, diag))
            if d < 2:
                fine.keep(S0, z, rb2[side, (6 + d) * FR : (7 + d) * FR, :])
    fine.seam(DA, -3)
    fine.seam(DA, FN + 2 - 7)
    fine.first_update(0)
    fine.first_update(FN - 1)
    for d in (1, 2):
        fine.first_update(-d, box_low)
        fine.first_update(FN - 1 + d, box_high)
    fine.seam(U1, -2)
    fine.seam(U1, FN + 1 - 7)
    fine.sweep(-1, box_low)
    fine.sweep(FN, box_high)
    for z in (0, 1, FN - 2, FN - 1):
        fine.sweep(z)
    fine.seam(U2, -1)
    fine.seam(U2, FN - 7)
    for z in (0, 1, 2):
        fine_finish(z)
    for z in (FN - 3, FN - 2, FN - 1):
        fine_finish(z)

    pl.when(has_up)(one_up.wait_send)
    pl.when(has_down)(one_down.wait_send)
    pl.when(has_up)(deep_up.wait_send)
    pl.when(has_down)(deep_down.wait_send)
    pl.when(s < subs - 1)(two_up.wait_send)
    pl.when(s > 0)(two_down.wait_send)


def place_kernel(
    fine_in, coarse_in, spot_in, fvel_hbm, fpres_hbm, cvel_hbm, cpres_hbm, fbuf, cbuf, sem
):
    copies = []

    def send(src, dst):
        copy = pltpu.make_async_copy(src, dst, sem.at[len(copies)])
        copy.start()
        copies.append(copy)

    for f in range(4):
        for z in range(FN):
            x = fine_in[f, z]
            fbuf[f, z, 0:FR, :] = x[:, 0:HALF]
            fbuf[f, z, FR : 2 * FR, :] = x[:, HALF:LANES]
        send(fbuf.at[f], fvel_hbm.at[f] if f < 3 else fpres_hbm)
    row = lax.broadcasted_iota(jnp.int32, (32, HALF), 0)
    col = lax.broadcasted_iota(jnp.int32, (32, HALF), 1)
    mean = jnp.where(row == col // 2, 0.125, 0.0).astype(BF16)
    lane = lane_of(32)
    covers = col // 32 == spot_in[0:1, 0:HALF]
    for f in range(4):
        pairs = []
        for k in range(CN):
            parts = [
                fbuf[f, z, pl.ds(start, FR, stride=2), :]
                for z in (2 * k, 2 * k + 1)
                for start in range(2)
            ]
            pairs.append((parts[0] + parts[1]) + (parts[2] + parts[3]))
        blk = pick_nt(mean, jnp.concatenate(pairs, axis=0))
        for k in range(CN):
            lo = pltpu.roll(blk, (LANES - 32 * k) % LANES, 1) if k else blk
            hi = pltpu.roll(blk, (LANES + 32 - 32 * k) % LANES, 1) if k != 1 else blk
            x = coarse_in[f, k]
            own = jnp.concatenate([x[:, 0:HALF], x[:, HALF:LANES]], axis=0)
            cbuf[f, k] = jnp.where(covers, jnp.where(lane < 32, lo, hi)[:, 0:HALF], own)
    send(cbuf.at[pl.ds(0, 3)], cvel_hbm)
    send(cbuf.at[3], cpres_hbm)
    for copy in copies:
        copy.wait()


def on_device(groups, subs, cu, cp, cm, cf, fu, fp, fm, ff, spots):
    cu, cf = [a.transpose(0, 1, 3, 2) for a in (cu, cf)]
    cp, cm = [a.transpose(0, 2, 1) for a in (cp, cm)]
    fu, ff = [a[:, :, 0] for a in (fu, ff)]
    fp, fm = [a[:, 0] for a in (fp, fm)]
    vmem = functools.partial(pltpu.VMEM, dtype=F32)
    smem_spec = pl.BlockSpec(memory_space=pltpu.SMEM)
    hbm_spec = pl.BlockSpec(memory_space=pltpu.HBM)
    vmem_spec = pl.BlockSpec(memory_space=pltpu.VMEM)
    fine, coarse, spot = pl.pallas_call(
        functools.partial(smooth_kernel, groups, subs),
        out_shape=(
            pltpu.VMEM((4, FN, FR, LANES), F32),
            pltpu.VMEM((4, CN, CR, LANES), F32),
            pltpu.VMEM((8, LANES), jnp.int32),
        ),
        in_specs=[smem_spec] + [hbm_spec] * 8,
        out_specs=(vmem_spec,) * 3,
        scratch_shapes=[vmem(a.shape) for a in (cu, cp, cm, cf, fu, fp, fm, ff)]
        + [
            [vmem(((FN + 2 * OFF) * (FR + 2 * TOP), LANES))] * 10,
            [vmem((FN + 2 * OFF, FR, LANES))] * FLAT,
            [vmem(((CN + 2 * OFF) * (CR + 2 * TOP), LANES))] * 10,
            [vmem((CN + 2 * OFF, CR, LANES))] * FLAT,
        ]
        + [vmem((2, r, LANES)) for r in (5 * FR, COARSE_ROWS, 8 * FR) for _ in range(2)]
        + [pltpu.SemaphoreType.DMA((n,)) for n in (14, 2, 2, 2, 2, 2, 2)],
        compiler_params=pltpu.CompilerParams(
            collective_id=0, has_side_effects=True, vmem_limit_bytes=62 * 1024 * 1024
        ),
        name="smooth",
    )(spots, cu, cp, cm, cf, fu, fp, fm, ff)
    fvel, fpres, cvel, cpres = pl.pallas_call(
        place_kernel,
        out_shape=tuple(jax.ShapeDtypeStruct(a.shape, F32) for a in (fu, fp, cu, cp)),
        in_specs=[vmem_spec] * 3,
        out_specs=(hbm_spec,) * 4,
        scratch_shapes=[
            vmem((4, FN, 2 * FR, HALF)),
            vmem((4, CN, 2 * CR, HALF)),
            pltpu.SemaphoreType.DMA((6,)),
        ],
        compiler_params=pltpu.CompilerParams(vmem_limit_bytes=16 * 1024 * 1024),
        name="place",
    )(fine, coarse, spot)
    return (
        cvel.transpose(0, 1, 3, 2),
        cpres.transpose(0, 2, 1),
        fvel[:, :, None],
        fpres[:, None],
    )


def solution(mesh):
    groups, subs = mesh.shape["boxgrp"], mesh.shape["sub"]
    zs = ("boxgrp", "sub")
    return jax.shard_map(
        functools.partial(on_device, groups, subs),
        mesh=mesh,
        in_specs=(
            P(None, zs, None, None),
            P(zs, None, None),
            P(zs, None, None),
            P(None, zs, None, None),
            P(None, "sub", "boxgrp", None, None),
            P("sub", "boxgrp", None, None),
            P("sub", "boxgrp", None, None),
            P(None, "sub", "boxgrp", None, None),
            P(),
        ),
        out_specs=(
            P(None, zs, None, None),
            P(zs, None, None),
            P(None, "sub", "boxgrp", None, None),
            P("sub", "boxgrp", None, None),
        ),
        check_vma=False,
    )
```
